128 devices in a mesh: tm: 32 (over z, y, x_hi), clip: 4 (over x_lo, core).
Axes of the slice: x: 4 (x_hi: 2, x_lo: 2; x = x_hi * 2 + x_lo), y: 4, z: 4, core: 2. Of those that a mesh axis runs over, the one named last changes fastest.
Arguments:
- student_query: bfloat16 [16384, 1024], P('tm', 'clip'), may hold values from -12 to 12
- teacher_key: bfloat16 [65536, 1024], P('tm', 'clip'), may hold values from -1000 to 1000
- teacher_value: bfloat16 [65536, 1024], P('tm', 'clip'), may hold values from -12 to 12
- clip_order: int32 [65536], replicated, may hold values from 0 to 65535, as said below
- band_start: int32 [512], P('tm'), may hold values from -16 to -1
- band_end: int32 [512], P('tm'), may hold values from 1 to 16
- output_weight: bfloat16 [1024, 1024], P('clip'), may hold values from -0.1875 to 0.1875
- cotangent: bfloat16 [16384, 1024], P('tm', 'clip'), may hold values from -6 to 6
Outputs:
- joined: bfloat16 [16384, 1024], P('tm', 'clip')
- grad_query: bfloat16 [16384, 1024], P('tm', 'clip')
- grad_output_weight: float32 [1024, 1024], P('clip')
The draws below stay inside these ranges and needn't reach their ends.
Inputs may be any that keep to these rules, and one draw needn't show every extreme that they name: clip_order is a permutation. For a time row t of time shard j = t // 2048, clip_order[t] % 2048 lies in [j * 64, (j + 1) * 64): every input shard holds exactly 64 rows of every time shard, as one run.
All inputs are finite; a program needn't handle non-finite values.
Results may differ from the reference program's by a relative error of at most 0.0094.
Values may be sent and summed in bfloat16 or wider, within the bound.
A program may use at most 128 MiB of HBM per device.

```python
import math
import jax
import jax.numpy as jnp
from jax import lax

D = 1024
HEADS = 16
HDIM = 64
SBLK = 32
TBLK = 128
TROWS_DEV = 2048
REACH = 16
TS = 16384
TT = 65536
NSB = 512


def shuffle_one(stream_piece):
    return jax.random.permutation(stream_piece, TROWS_DEV)


def order_table(base_key):
    stream = jax.random.fold_in(base_key, 5)
    shard_count = TT // TROWS_DEV
    streams = jax.random.split(stream, shard_count)
    shuffled = jax.vmap(shuffle_one)(streams).astype(jnp.int32)
    portion = TROWS_DEV // shard_count
    target = jnp.arange(shard_count, dtype=jnp.int32)[:, None]
    placed = shuffled // portion * TROWS_DEV + target * portion + shuffled % portion
    return placed.reshape(TT).astype(jnp.int32)


def query_table(base_key):
    stream = jax.random.fold_in(base_key, 11)
    return jnp.clip(2.0 * jax.random.normal(stream, (TS, D), jnp.float32), -12.0, 12.0)


def band_table(base_key):
    streams = jax.random.split(jax.random.fold_in(base_key, 3), 5)
    regions = NSB // REACH
    region_width = jax.random.randint(streams[0], (regions,), 1, REACH + 1)
    block_width = jnp.repeat(region_width, REACH, total_repeat_length=NSB)
    starts = -(1 + jax.random.randint(streams[1], (NSB,), 0, 1 << 20) % block_width)
    ends = 1 + jax.random.randint(streams[2], (NSB,), 0, 1 << 20) % block_width
    blocks = jnp.arange(NSB, dtype=jnp.int32)
    starts = jnp.where(blocks == jax.random.randint(streams[3], (), 0, NSB), -REACH, starts)
    ends = jnp.where(blocks == jax.random.randint(streams[4], (), 0, NSB), REACH, ends)
    return (starts.astype(jnp.int32), ends.astype(jnp.int32))


def draw_student_query(key, part):
    return query_table(key).astype(jnp.bfloat16)


def draw_clip_order(key, part):
    return order_table(key)


def draw_band_start(key, part):
    return band_table(key)[0]


def draw_band_end(key, part):
    return band_table(key)[1]


def draw_teacher_key(key, part):
    stream = jax.random.fold_in(key, 13)
    return jnp.clip(jax.random.normal(stream, (TT, D), jnp.float32), -6.0, 6.0).astype(jnp.bfloat16)


def block_levels(key, shape, pieces, low, top_value):
    def one(position, shards_of):
        heights = jax.random.uniform(jax.random.fold_in(jax.random.fold_in(key, 6), position), (shards_of,), jnp.float32, low / len(pieces), top_value / len(pieces))
        return jnp.repeat(jnp.exp(heights), shape[position] // shards_of).reshape((-1,) + (1,) * (len(shape) - position - 1))

    gain = one(*pieces[0])
    for cut in pieces[1:]:
        gain = gain * one(*cut)
    return gain


def centred(stream_key, shape, scale, reach, cuts=(), kind=jnp.bfloat16):
    loudness = block_levels(stream_key, shape, cuts, -0.22, 0.18) if cuts else 1.0
    values = jax.random.normal(stream_key, shape, jnp.float32) * scale * loudness
    return jnp.minimum(jnp.maximum(values, -reach), reach).astype(kind)


def setup_inputs(seed: int = 0) -> dict:
    splits = jax.random.split(jax.random.key(seed), 9)
    student_query = draw_student_query(jax.random.fold_in(splits[8], 71), 0)
    teacher_key = draw_teacher_key(jax.random.fold_in(splits[8], 71), 0)
    teacher_value = centred(splits[2], (TT, D), 2.0, 12.0, ((0, 32), (1, 4)))
    clip_order = draw_clip_order(jax.random.fold_in(splits[8], 71), 0)
    band_start = draw_band_start(jax.random.fold_in(splits[8], 71), 0)
    band_end = draw_band_end(jax.random.fold_in(splits[8], 71), 0)
    output_weight = centred(splits[6], (D, D), D ** -0.5, 0.1875, ((0, 4),))
    cotangent = centred(splits[7], (TS, D), 1.0, 6.0, ((0, 32), (1, 4)))
    return {"student_query": student_query, "teacher_key": teacher_key, "teacher_value": teacher_value, "clip_order": clip_order, "band_start": band_start, "band_end": band_end, "output_weight": output_weight, "cotangent": cotangent}


def reference(student_query, teacher_key, teacher_value, clip_order, band_start, band_end, output_weight, cotangent):
    key_time = teacher_key[clip_order]
    value_time = teacher_value[clip_order]
    margin = REACH * TBLK
    key_wide = jnp.pad(key_time, ((margin, margin), (0, 0)))
    value_wide = jnp.pad(value_time, ((margin, margin), (0, 0)))
    attn_grad = jnp.dot(cotangent, output_weight.T, preferred_element_type=jnp.float32).astype(jnp.bfloat16)
    window = (2 * REACH + 1) * TBLK
    scaling = 1.0 / math.sqrt(HDIM)

    def one_block(inputs):
        block_index, query_rows, grad_rows, start_off, end_off = inputs
        anchor = (block_index * TBLK).astype(jnp.int32)
        key_part = lax.dynamic_slice(key_wide, (anchor, jnp.int32(0)), (window, D)).astype(jnp.float32).reshape(window, HEADS, HDIM)
        value_part = lax.dynamic_slice(value_wide, (anchor, jnp.int32(0)), (window, D)).astype(jnp.float32).reshape(window, HEADS, HDIM)
        query_part = query_rows.astype(jnp.float32).reshape(SBLK, HEADS, HDIM)
        scores = jnp.einsum('qhd,khd->hqk', query_part, key_part) * scaling
        key_block = block_index - REACH + jnp.arange(window, dtype=jnp.int32) // TBLK
        valid = (key_block >= block_index + start_off) & (key_block <= block_index + end_off)
        valid = valid & (key_block >= 0) & (key_block < NSB)
        scores = jnp.where(valid[None, None, :], scores, -jnp.inf)
        row_max = lax.optimization_barrier(jnp.max(scores, axis=-1, keepdims=True))
        shifted = jnp.exp(scores - row_max)
        probs = shifted / lax.optimization_barrier(jnp.sum(shifted, axis=-1, keepdims=True))
        weights = lax.optimization_barrier(probs.astype(jnp.bfloat16)).astype(jnp.float32)
        head_out = jnp.einsum('hqk,khd->qhd', weights, value_part).astype(jnp.bfloat16)
        grad_part = grad_rows.astype(jnp.float32).reshape(SBLK, HEADS, HDIM)
        dprobs = jnp.einsum('qhd,khd->hqk', grad_part, value_part)
        delta = lax.optimization_barrier(jnp.sum(probs * dprobs, axis=-1, keepdims=True))
        dscores = lax.optimization_barrier((probs * (dprobs - delta) * scaling).astype(jnp.bfloat16)).astype(jnp.float32)
        query_grad = jnp.einsum('hqk,khd->qhd', dscores, key_part).astype(jnp.bfloat16)
        return (head_out.reshape(SBLK, D), query_grad.reshape(SBLK, D))
    attention, grad_query = lax.map(one_block, (jnp.arange(NSB, dtype=jnp.int32), student_query.reshape(NSB, SBLK, D), attn_grad.reshape(NSB, SBLK, D), band_start, band_end))
    attention = attention.reshape(TS, D)
    grad_query = grad_query.reshape(TS, D)
    joined = jnp.dot(attention, output_weight, preferred_element_type=jnp.float32).astype(jnp.bfloat16)
    grad_output_weight = jnp.dot(attention.T, cotangent, preferred_element_type=jnp.float32)
    return (joined, grad_query, grad_output_weight)
```

```python
import functools
import math

import jax
import jax.numpy as jnp
from jax import lax
from jax.experimental import pallas as pl
from jax.experimental.pallas import tpu as pltpu
from jax.sharding import PartitionSpec as P

HDIM = 64
SBLK = 32
TBLK = 128
F = 128
CH = 256
ANY = pl.BlockSpec(memory_space=pl.ANY)
MESH = pl.DeviceIdType.MESH


def greet(shards, groups):
    me = lax.axis_index("tm")
    c = lax.axis_index("clip")
    barrier = pltpu.get_barrier_semaphore()

    def tell(d, carry):
        pl.semaphore_signal(
            barrier, inc=1, device_id={"tm": lax.rem(me + d, shards)}, device_id_type=MESH
        )
        return carry

    lax.fori_loop(1, shards, tell, 0)
    for d in range(1, groups):
        pl.semaphore_signal(
            barrier, inc=1, device_id={"clip": lax.rem(c + d, groups)}, device_id_type=MESH
        )
    pl.semaphore_wait(barrier, shards + groups - 2)


def scatter_kernel(
    shards, groups, tk, tv, sq, cot, ow, kv, cotf, wcols, qp,
    ks, kr, vs, vr, cs, cr, ws, wr, qs, qr, ls,
):
    me = lax.axis_index("tm")
    c = lax.axis_index("clip")
    half = lax.rem(me, 2)
    mate = me + 1 - 2 * half
    wide = cot.shape[1]
    greet(shards, groups)

    def key_copy(target, slot, src):
        p = lax.div(target, 2)
        col = pl.multiple_of(lax.rem(target, 2) * 128, 128)
        return (
            pltpu.make_async_remote_copy(
                src_ref=tk.at[pl.ds(2 * p, 2), :, pl.ds(col, 128)],
                dst_ref=kv.at[:, me, :, pl.ds(0, 128)],
                send_sem=ks.at[slot],
                recv_sem=kr.at[src],
                device_id={"tm": target},
                device_id_type=MESH,
            ),
            pltpu.make_async_remote_copy(
                src_ref=tv.at[pl.ds(2 * p, 2), :, pl.ds(col, 128)],
                dst_ref=kv.at[:, me, :, pl.ds(128, 128)],
                send_sem=vs.at[slot],
                recv_sem=vr.at[src],
                device_id={"tm": target},
                device_id_type=MESH,
            ),
        )

    def clip_copy(d, src):
        target = lax.rem(c + d, groups)
        mine = pl.multiple_of(c * wide, 128)
        theirs = pl.multiple_of(target * wide, 128)
        return (
            pltpu.make_async_remote_copy(
                src_ref=cot,
                dst_ref=cotf.at[:, pl.ds(mine, wide)],
                send_sem=cs.at[d],
                recv_sem=cr.at[src],
                device_id={"clip": target},
                device_id_type=MESH,
            ),
            pltpu.make_async_remote_copy(
                src_ref=ow.at[:, pl.ds(theirs, wide)],
                dst_ref=wcols.at[c],
                send_sem=ws.at[d],
                recv_sem=wr.at[src],
                device_id={"clip": target},
                device_id_type=MESH,
            ),
        )

    other = pl.multiple_of((1 - half) * 128, 128)
    own = pl.multiple_of(half * 128, 128)
    q_copy = pltpu.make_async_remote_copy(
        src_ref=sq.at[:, pl.ds(other, 128)],
        dst_ref=qp.at[half],
        send_sem=qs,
        recv_sem=qr,
        device_id={"tm": mate},
        device_id_type=MESH,
    )

    def start(d, carry):
        for copy in key_copy(lax.rem(me + d, shards), d, me):
            copy.start()
        return carry

    lax.fori_loop(1, shards, start, 0)
    for d in range(1, groups):
        for copy in clip_copy(d, c):
            copy.start()
    q_copy.start()
    mine = pl.multiple_of(c * wide, 128)
    pair = lax.div(me, 2)
    local = (
        pltpu.make_async_copy(
            tk.at[pl.ds(2 * pair, 2), :, pl.ds(own, 128)], kv.at[:, me, :, pl.ds(0, 128)], ls.at[0]
        ),
        pltpu.make_async_copy(
            tv.at[pl.ds(2 * pair, 2), :, pl.ds(own, 128)], kv.at[:, me, :, pl.ds(128, 128)], ls.at[1]
        ),
        pltpu.make_async_copy(cot, cotf.at[:, pl.ds(mine, wide)], ls.at[2]),
        pltpu.make_async_copy(ow.at[:, pl.ds(mine, wide)], wcols.at[c], ls.at[3]),
        pltpu.make_async_copy(sq.at[:, pl.ds(own, 128)], qp.at[half], ls.at[4]),
    )
    for copy in local:
        copy.start()

    def finish(d, carry):
        for copy in key_copy(lax.rem(me + d, shards), d, lax.rem(me + d, shards)):
            copy.wait()
        return carry

    for copy in local:
        copy.wait()
    q_copy.wait()
    for d in range(1, groups):
        for copy in clip_copy(d, lax.rem(c + d, groups)):
            copy.wait()
    lax.fori_loop(1, shards, finish, 0)


def scatter(tk, tv, sq, cot, ow, shards, groups):
    bf = jnp.bfloat16
    rows, wide = sq.shape
    dma = pltpu.SemaphoreType.DMA
    return pl.pallas_call(
        functools.partial(scatter_kernel, shards, groups),
        out_shape=(
            jax.ShapeDtypeStruct((2, shards, 64, 256), bf),
            jax.ShapeDtypeStruct((rows, groups * wide), bf),
            jax.ShapeDtypeStruct((groups, wide, wide), bf),
            jax.ShapeDtypeStruct((2, rows, 128), bf),
        ),
        in_specs=[ANY] * 5,
        out_specs=(ANY,) * 4,
        scratch_shapes=[
            dma((shards,)), dma((shards,)), dma((shards,)), dma((shards,)),
            dma((groups,)), dma((groups,)), dma((groups,)), dma((groups,)),
            dma(()), dma(()), dma((5,)),
        ],
        compiler_params=pltpu.CompilerParams(collective_id=0, has_side_effects=True),
        name="scatter",
    )(tk, tv, sq, cot, ow)


def sort_kernel(idx_ref, kv_ref, out_ref):
    i = pl.program_id(0)
    depth = kv_ref.shape[0]
    lane = lax.broadcasted_iota(jnp.int32, (128, 128), 1)
    for r in range(2):
        row = idx_ref[pl.ds(2 * i + r, 1), :]
        col = jnp.broadcast_to(row, (128, 128)).T
        hot = jnp.concatenate(
            [
                jnp.where(col == lane + 128 * k, 1.0, 0.0).astype(jnp.bfloat16)
                for k in range(depth // 128)
            ],
            axis=1,
        )
        out_ref[r * 128 : (r + 1) * 128, :] = jnp.dot(
            hot, kv_ref[...], preferred_element_type=jnp.float32
        ).astype(jnp.bfloat16)


def sort_rows(idx, kv):
    total = kv.shape[0]
    half = total // 2
    steps = total // 256
    per = half // 256
    return pl.pallas_call(
        sort_kernel,
        grid=(steps,),
        out_shape=jax.ShapeDtypeStruct((total, 256), jnp.bfloat16),
        in_specs=[
            pl.BlockSpec((total // 128, 128), lambda i: (0, 0)),
            pl.BlockSpec((half, 256), lambda i: (i // per, 0)),
        ],
        out_specs=pl.BlockSpec((256, 256), lambda i: (i, 0)),
        cost_estimate=pl.CostEstimate(
            flops=2 * total * half * 256, bytes_accessed=4 * total * 256, transcendentals=0
        ),
        name="sort_rows",
    )(idx, kv)


def attend_kernel(
    lo_ref, hi_ref, left, own, right, q_ref, g_ref, out_ref,
    kv, s_scr, d_scr, qb, gb, m_scr, l_scr, dd_scr, o_scr, sem,
):
    i = pl.program_id(0)
    side = left.shape[0]
    mid = own.shape[0]

    @pl.when(i == 0)
    def _():
        copies = (
            pltpu.make_async_copy(left, kv.at[pl.ds(0, side)], sem.at[0]),
            pltpu.make_async_copy(own, kv.at[pl.ds(side, mid)], sem.at[1]),
            pltpu.make_async_copy(right, kv.at[pl.ds(side + mid, side)], sem.at[2]),
        )
        for copy in copies:
            copy.start()
        for copy in copies:
            copy.wait()

    nb = F // SBLK
    los = [lo_ref[nb * i + r] for r in range(nb)]
    his = [hi_ref[nb * i + r] for r in range(nb)]
    low = functools.reduce(jnp.minimum, los)
    high = functools.reduce(jnp.maximum, his)
    per = CH // TBLK
    first = low // per
    count = high // per - first + 1

    lane = lax.broadcasted_iota(jnp.int32, (F, 128), 1)
    zero = jnp.zeros((F, 128), jnp.bfloat16)
    q = q_ref[...] * jnp.bfloat16(0.125)
    g = g_ref[...]
    qb[0:F, :] = jnp.where(lane < HDIM, q, zero)
    qb[F : 2 * F, :] = jnp.where(lane < HDIM, zero, q)
    gb[0:F, :] = jnp.where(lane < HDIM, g, zero)
    gb[F : 2 * F, :] = jnp.where(lane < HDIM, zero, g)
    m_scr[...] = jnp.full_like(m_scr, -jnp.inf)
    l_scr[...] = jnp.zeros_like(l_scr)
    dd_scr[...] = jnp.zeros_like(dd_scr)
    o_scr[...] = jnp.zeros_like(o_scr)
    nt = (((1,), (1,)), ((), ()))

    def first_pass(k, carry):
        base = pl.multiple_of((first + k) * CH, CH)
        keys = kv[pl.ds(base, CH), 0:128]
        values = kv[pl.ds(base, CH), 128:256]
        scores = lax.dot_general(qb[...], keys, nt, preferred_element_type=jnp.float32)
        for r in range(nb):
            for c in range(per):
                block = (first + k) * per + c
                ok = (block >= los[r]) & (block <= his[r])
                bias = jnp.where(ok, 0.0, -jnp.inf).astype(jnp.float32)
                for h in range(2):
                    a = h * F + r * SBLK
                    part = scores[a : a + SBLK, c * 128 : (c + 1) * 128] + bias
                    s_scr[k, a : a + SBLK, c * 128 : (c + 1) * 128] = part
                    m_scr[a : a + SBLK, :] = jnp.maximum(m_scr[a : a + SBLK, :], part)
        d_scr[k] = lax.dot_general(gb[...], values, nt, preferred_element_type=jnp.float32)
        return carry

    lax.fori_loop(0, count, first_pass, 0)
    m_scr[...] = jnp.broadcast_to(jnp.max(m_scr[...], axis=1, keepdims=True), m_scr.shape)

    def second_pass(k, carry):
        base = pl.multiple_of((first + k) * CH, CH)
        values = kv[pl.ds(base, CH), 128:256]
        top = m_scr[...]
        parts = []
        for c in range(per):
            part = jnp.exp(s_scr[k, :, c * 128 : (c + 1) * 128] - top)
            s_scr[k, :, c * 128 : (c + 1) * 128] = part
            l_scr[...] += part
            dd_scr[...] += part * d_scr[k, :, c * 128 : (c + 1) * 128]
            parts.append(part.astype(jnp.bfloat16))
        weights = jnp.concatenate(parts, axis=1)
        o_scr[...] += jnp.dot(weights, values, preferred_element_type=jnp.float32)
        return carry

    lax.fori_loop(0, count, second_pass, 0)
    inv = 1.0 / jnp.sum(l_scr[...], axis=1, keepdims=True)
    delta = jnp.sum(dd_scr[...], axis=1, keepdims=True) * inv
    m_scr[...] = jnp.broadcast_to(delta, m_scr.shape)
    l_scr[...] = jnp.broadcast_to(inv, l_scr.shape)
    out = o_scr[...] * l_scr[...]
    out_ref[:, 0:128] = jnp.where(lane < HDIM, out[0:F], out[F : 2 * F]).astype(jnp.bfloat16)
    o_scr[...] = jnp.zeros_like(o_scr)

    def third_pass(k, carry):
        base = pl.multiple_of((first + k) * CH, CH)
        keys = kv[pl.ds(base, CH), 0:128]
        centre = m_scr[...]
        parts = []
        for c in range(per):
            part = s_scr[k, :, c * 128 : (c + 1) * 128] * (
                d_scr[k, :, c * 128 : (c + 1) * 128] - centre
            )
            parts.append(part.astype(jnp.bfloat16))
        o_scr[...] += jnp.dot(
            jnp.concatenate(parts, axis=1), keys, preferred_element_type=jnp.float32
        )
        return carry

    lax.fori_loop(0, count, third_pass, 0)
    out = o_scr[...] * (l_scr[...] * 0.125)
    out_ref[:, 128:256] = jnp.where(lane < HDIM, out[0:F], out[F : 2 * F]).astype(jnp.bfloat16)


def attend(lo, hi, left, own, right, q, g):
    frames = q.shape[0]
    window = 2 * left.shape[0] + own.shape[0]
    reach = left.shape[0] // TBLK
    chunks = (2 * reach + F // SBLK) * TBLK // CH + 2
    f32 = jnp.float32
    return pl.pallas_call(
        attend_kernel,
        grid_spec=pltpu.PrefetchScalarGridSpec(
            num_scalar_prefetch=2,
            grid=(frames // F,),
            in_specs=[
                ANY, ANY, ANY,
                pl.BlockSpec((F, 128), lambda i, lo, hi: (i, 0)),
                pl.BlockSpec((F, 128), lambda i, lo, hi: (i, 0)),
            ],
            out_specs=pl.BlockSpec((F, 256), lambda i, lo, hi: (i, 0)),
            scratch_shapes=[
                pltpu.VMEM((window, 256), jnp.bfloat16),
                pltpu.VMEM((chunks, 2 * F, CH), f32),
                pltpu.VMEM((chunks, 2 * F, CH), f32),
                pltpu.VMEM((2 * F, 128), jnp.bfloat16),
                pltpu.VMEM((2 * F, 128), jnp.bfloat16),
                pltpu.VMEM((2 * F, 128), f32),
                pltpu.VMEM((2 * F, 128), f32),
                pltpu.VMEM((2 * F, 128), f32),
                pltpu.VMEM((2 * F, 128), f32),
                pltpu.SemaphoreType.DMA((3,)),
            ],
        ),
        out_shape=jax.ShapeDtypeStruct((frames, 256), jnp.bfloat16),
        cost_estimate=pl.CostEstimate(
            flops=8 * frames * 4096 * 256, bytes_accessed=6 << 20, transcendentals=frames * 8192
        ),
        name="attend",
    )(lo, hi, left, own, right, q, g)


def reduce_kernel(
    shards, groups, wg, o_ref, wsum, og, got, red, ss, sr, gs, gr, os_, or_, ls,
):
    me = lax.axis_index("tm")
    c = lax.axis_index("clip")
    wide = o_ref.shape[1]
    greet(shards, groups)

    def part_copy(target, slot, src):
        return pltpu.make_async_remote_copy(
            src_ref=wg.at[target],
            dst_ref=got.at[me],
            send_sem=ss.at[slot],
            recv_sem=sr.at[src],
            device_id={"tm": target},
            device_id_type=MESH,
        )

    def sum_copy(target, slot, src):
        return pltpu.make_async_remote_copy(
            src_ref=red,
            dst_ref=wsum.at[me],
            send_sem=gs.at[slot],
            recv_sem=gr.at[src],
            device_id={"tm": target},
            device_id_type=MESH,
        )

    def o_copy(d, src):
        mine = pl.multiple_of(c * wide, 128)
        return pltpu.make_async_remote_copy(
            src_ref=o_ref,
            dst_ref=og.at[:, pl.ds(mine, wide)],
            send_sem=os_.at[d],
            recv_sem=or_.at[src],
            device_id={"clip": lax.rem(c + d, groups)},
            device_id_type=MESH,
        )

    def start(d, carry):
        part_copy(lax.rem(me + d, shards), d, me).start()
        return carry

    def finish(d, carry):
        part_copy(lax.rem(me + d, shards), d, lax.rem(me + d, shards)).wait()
        return carry

    def start_sum(d, carry):
        sum_copy(lax.rem(me + d, shards), d, me).start()
        return carry

    def finish_sum(d, carry):
        sum_copy(lax.rem(me + d, shards), d, lax.rem(me + d, shards)).wait()
        return carry

    own = pltpu.make_async_copy(wg.at[me], got.at[me], ls.at[0])
    own.start()
    lax.fori_loop(1, shards, start, 0)
    for d in range(1, groups):
        o_copy(d, c).start()
    mine = pl.multiple_of(c * wide, 128)
    own_o = pltpu.make_async_copy(o_ref, og.at[:, pl.ds(mine, wide)], ls.at[1])
    own_o.start()
    own.wait()
    lax.fori_loop(1, shards, finish, 0)

    def add(s, acc):
        return acc + got[s].astype(jnp.float32)

    red[...] = lax.fori_loop(
        0, shards, add, jnp.zeros(red.shape, jnp.float32)
    ).astype(jnp.bfloat16)
    lax.fori_loop(1, shards, start_sum, 0)
    own_sum = pltpu.make_async_copy(red, wsum.at[me], ls.at[2])
    own_sum.start()
    own_o.wait()
    for d in range(1, groups):
        o_copy(d, lax.rem(c + d, groups)).wait()
    own_sum.wait()
    lax.fori_loop(1, shards, finish_sum, 0)


def reduce_all(wg, o, shards, groups):
    bf = jnp.bfloat16
    dma = pltpu.SemaphoreType.DMA
    _, part, cols = wg.shape
    rows, wide = o.shape
    return pl.pallas_call(
        functools.partial(reduce_kernel, shards, groups),
        out_shape=(
            jax.ShapeDtypeStruct((shards, part, cols), bf),
            jax.ShapeDtypeStruct((rows, groups * wide), bf),
        ),
        in_specs=[ANY] * 2,
        out_specs=(ANY,) * 2,
        scratch_shapes=[
            pltpu.VMEM((shards, part, cols), bf),
            pltpu.VMEM((part, cols), bf),
            dma((shards,)), dma((shards,)), dma((shards,)), dma((shards,)),
            dma((groups,)), dma((groups,)), dma((3,)),
        ],
        compiler_params=pltpu.CompilerParams(collective_id=1, has_side_effects=True),
        name="reduce_all",
    )(wg, o)


def on_device(
    student_query,
    teacher_key,
    teacher_value,
    clip_order,
    band_start,
    band_end,
    output_weight,
    cotangent,
):
    shards = lax.axis_size("tm")
    groups = lax.axis_size("clip")
    me = lax.axis_index("tm")
    half = me % 2
    pair = me // 2
    rows, wide = student_query.shape
    trows = teacher_key.shape[0]
    piece = trows // shards
    blocks = rows // SBLK
    f32 = jnp.float32
    bf = jnp.bfloat16

    kv, cot_full, w_cols, q_pair = scatter(
        teacher_key.reshape(shards, piece, wide),
        teacher_value.reshape(shards, piece, wide),
        student_query, cotangent, output_weight, shards, groups,
    )

    lookup = lax.dynamic_slice_in_dim(clip_order, pair * 2 * trows, 2 * trows)
    idx = lookup // trows * piece + lookup % piece
    own = sort_rows(idx.reshape(2 * trows // 128, 128), kv.reshape(2 * trows, 256))

    up = [(i, i + 2) for i in range(shards - 2)]
    down = [(i + 2, i) for i in range(shards - 2)]
    swap = [(i, i ^ 1) for i in range(shards)]
    left = lax.ppermute(own[trows:], "tm", up)
    right = lax.ppermute(own[:trows], "tm", down)

    grad = lax.dot_general(
        cot_full, output_weight, (((1,), (1,)), ((), ())), preferred_element_type=f32
    ).astype(bf)
    grad_own = lax.dynamic_slice_in_dim(grad, half * 128, 128, axis=1)
    grad_mate = lax.ppermute(
        lax.dynamic_slice_in_dim(grad, (1 - half) * 128, 128, axis=1), "tm", swap
    )
    first = half == 0
    g_pair = jnp.concatenate(
        [jnp.where(first, grad_own, grad_mate), jnp.where(first, grad_mate, grad_own)], axis=0
    )

    bands = jnp.stack([band_start, band_end])
    bands_mate = lax.ppermute(bands, "tm", swap)
    bands = jnp.concatenate(
        [jnp.where(first, bands, bands_mate), jnp.where(first, bands_mate, bands)], axis=1
    )
    reach = trows // TBLK
    base = pair * 2 * blocks
    at = reach + jnp.arange(2 * blocks, dtype=jnp.int32)
    total = shards * blocks
    lo = jnp.maximum(at + bands[0], reach - base)
    hi = jnp.minimum(at + bands[1], total - 1 + reach - base)

    od = attend(lo, hi, left, own, right, q_pair.reshape(2 * rows, 128), g_pair)

    mine = lax.dynamic_slice_in_dim(od, half * rows, rows, axis=0)
    back = lax.ppermute(
        lax.dynamic_slice_in_dim(od, (1 - half) * rows, rows, axis=0), "tm", swap
    )
    lower = jnp.where(first, mine, back)
    upper = jnp.where(first, back, mine)
    attention = jnp.concatenate([lower[:, :128], upper[:, :128]], axis=1)
    grad_query = jnp.concatenate([lower[:, 128:], upper[:, 128:]], axis=1)

    local = lax.dot_general(
        attention, cot_full, (((0,), (0,)), ((), ())), preferred_element_type=f32
    ).astype(bf)
    wsum, o_full = reduce_all(
        local.reshape(shards, wide // shards, groups * wide), attention, shards, groups
    )
    joined = jnp.dot(
        o_full, w_cols.reshape(groups * wide, wide), preferred_element_type=f32
    ).astype(bf)
    weight_grad = wsum.reshape(wide, groups * wide).astype(f32)
    return (joined, grad_query, weight_grad)


def solution(mesh):
    return jax.shard_map(
        on_device,
        mesh=mesh,
        in_specs=(
            P("tm", "clip"),
            P("tm", "clip"),
            P("tm", "clip"),
            P(),
            P("tm"),
            P("tm"),
            P("clip", None),
            P("tm", "clip"),
        ),
        out_specs=(P("tm", "clip"), P("tm", "clip"), P("clip", None)),
        check_vma=False,
    )
```

```python
import functools
import math

import jax
import jax.numpy as jnp
from jax import lax
from jax.experimental import pallas as pl
from jax.experimental.pallas import tpu as pltpu
from jax.sharding import PartitionSpec as P

HDIM = 64
SBLK = 32
TBLK = 128
F = 128
CH = 1024
GROUP = 1024
ANY = pl.BlockSpec(memory_space=pl.ANY)
MESH = pl.DeviceIdType.MESH


def greet(shards, bits):
    me = lax.axis_index("tm")
    c = lax.axis_index("clip")
    barrier = pltpu.get_barrier_semaphore()

    def tell(d, carry):
        pl.semaphore_signal(
            barrier, inc=1, device_id={"tm": lax.rem(me + d, shards)}, device_id_type=MESH
        )
        return carry

    lax.fori_loop(1, shards, tell, 0)
    for bit in bits:
        pl.semaphore_signal(
            barrier, inc=1, device_id={"clip": flip(c, bit)}, device_id_type=MESH
        )
    pl.semaphore_wait(barrier, shards - 1 + len(bits))


def flip(c, bit):
    if bit == 3:
        return 3 - c
    return c + bit - 2 * bit * lax.rem(lax.div(c, bit), 2)


def send(src, dst, sems, **where):
    return pltpu.make_async_remote_copy(
        src_ref=src, dst_ref=dst, send_sem=sems[0], recv_sem=sems[1],
        device_id=where, device_id_type=MESH,
    )


def exchange_kernel(
    shards, tk, tv, sq, cot, ow, bands,
    kv, left, right, cotf, wcols, qp, gp, bp,
    cotv, wv, gv, ks, kr, vs, vr, ls, lr, rs, rr, cs, ws, wr, ms, os_,
):
    me = lax.axis_index("tm")
    c = lax.axis_index("clip")
    half = lax.rem(me, 2)
    mate = flip(me, 1)
    pair = lax.div(me, 2)
    groups, rows, wide = cotv.shape
    near, far = flip(c, 1), flip(c, 2)
    across = flip(far, 1)
    prev = lax.rem(me + shards - 2, shards)
    after = lax.rem(me + 2, shards)
    greet(shards, (1, 2, 3))

    def key_copies(target, slot, src):
        p = lax.div(target, 2)
        col = pl.multiple_of(lax.rem(target, 2) * 128, 128)
        return (
            send(
                tk.at[pl.ds(2 * p, 2), :, pl.ds(col, 128)],
                kv.at[:, me, :, pl.ds(0, 128)], (ks.at[slot], kr.at[src]), tm=target,
            ),
            send(
                tv.at[pl.ds(2 * p, 2), :, pl.ds(col, 128)],
                kv.at[:, me, :, pl.ds(128, 128)], (vs.at[slot], vr.at[src]), tm=target,
            ),
        )

    def halo_copies(s):
        return (
            send(kv.at[0, s], right.at[s], (rs.at[s], rr.at[s]), tm=prev),
            send(kv.at[1, s], left.at[s], (ls.at[s], lr.at[s]), tm=after),
        )

    def w_copy(d, src):
        target = lax.rem(c + d, groups)
        theirs = pl.multiple_of(target * wide, 128)
        return send(
            ow.at[:, pl.ds(theirs, wide)], wcols.at[c], (ws.at[d], wr.at[src]), clip=target
        )

    own = pl.multiple_of(half * 128, 128)
    other = pl.multiple_of((1 - half) * 128, 128)
    mine = pl.multiple_of(c * wide, 128)
    cot_far = send(cot, cotv.at[c], (cs.at[0], cs.at[1]), clip=far)
    cot_near = send(cot, cotv.at[c], (cs.at[2], cs.at[3]), clip=near)
    cot_relay = send(cotv.at[far], cotv.at[far], (cs.at[4], cs.at[5]), clip=near)
    q_copy = send(sq.at[:, pl.ds(other, 128)], qp.at[half], (ms.at[0], ms.at[1]), tm=mate)
    b_copy = send(bands, bp.at[half], (ms.at[2], ms.at[3]), tm=mate)
    g_copy = send(gv.at[1 - half], gp.at[half], (ms.at[4], ms.at[5]), tm=mate)

    cot_far.start()
    cot_near.start()

    def start(d, carry):
        for copy in key_copies(lax.rem(me + d, shards), d, me):
            copy.start()
        return carry

    lax.fori_loop(1, shards, start, 0)
    q_copy.start()
    b_copy.start()
    for d in range(1, groups):
        w_copy(d, c).start()
    mine_kv = (
        pltpu.make_async_copy(
            tk.at[pl.ds(2 * pair, 2), :, pl.ds(own, 128)], kv.at[:, me, :, pl.ds(0, 128)], os_.at[0]
        ),
        pltpu.make_async_copy(
            tv.at[pl.ds(2 * pair, 2), :, pl.ds(own, 128)], kv.at[:, me, :, pl.ds(128, 128)], os_.at[1]
        ),
    )
    mine_cot = (
        pltpu.make_async_copy(cot, cotv.at[c], os_.at[2]),
        pltpu.make_async_copy(ow, wv, os_.at[3]),
    )
    mine_rest = (
        pltpu.make_async_copy(ow.at[:, pl.ds(mine, wide)], wcols.at[c], os_.at[4]),
        pltpu.make_async_copy(sq.at[:, pl.ds(own, 128)], qp.at[half], os_.at[5]),
        pltpu.make_async_copy(bands, bp.at[half], os_.at[6]),
    )
    for copy in mine_cot + mine_kv + mine_rest:
        copy.start()
    for copy in mine_cot + mine_kv:
        copy.wait()
    for copy in halo_copies(me):
        copy.start()
    cot_far.wait_recv()
    cot_relay.start()
    cot_near.wait_recv()
    cot_relay.wait_recv()
    nt = (((1,), (1,)), ((), ()))
    grad = jnp.zeros((rows, wide), jnp.float32)
    for j in range(groups):
        grad += lax.dot_general(
            cotv[j], wv[:, j * wide : (j + 1) * wide], nt, preferred_element_type=jnp.float32
        )
    gv[0] = grad[:, 0:128].astype(jnp.bfloat16)
    gv[1] = grad[:, 128:256].astype(jnp.bfloat16)
    put_cot = pltpu.make_async_copy(cotv, cotf, os_.at[7])
    put_cot.start()

    def forward(d, carry):
        s = lax.rem(me + shards - d, shards)
        for copy in key_copies(lax.rem(me + d, shards), d, s):
            copy.wait_recv()
        for copy in halo_copies(s):
            copy.start()
        return carry

    lax.fori_loop(1, 3, forward, 0)
    g_copy.start()
    put_g = pltpu.make_async_copy(gv.at[half], gp.at[half], os_.at[8])
    put_g.start()
    lax.fori_loop(3, shards, forward, 0)

    def finish(d, carry):
        s = lax.rem(me + shards - d, shards)
        for copy in key_copies(lax.rem(me + d, shards), d, s):
            copy.wait_send()
        return carry

    lax.fori_loop(1, shards, finish, 0)
    for copy in mine_rest:
        copy.wait()
    put_cot.wait()
    put_g.wait()
    cot_far.wait_send()
    cot_near.wait_send()
    cot_relay.wait_send()
    q_copy.wait()
    b_copy.wait()
    g_copy.wait()
    for d in range(1, groups):
        w_copy(d, lax.rem(c + groups - d, groups)).wait()

    def arrive(s, carry):
        for copy in halo_copies(s):
            copy.wait()
        return carry

    lax.fori_loop(0, shards, arrive, 0)


def exchange(tk, tv, sq, cot, ow, bands, shards, groups):
    bf = jnp.bfloat16
    rows, wide = sq.shape
    piece = tk.shape[1]
    dma = pltpu.SemaphoreType.DMA
    halo = jax.ShapeDtypeStruct((shards, piece, 256), bf)
    return pl.pallas_call(
        functools.partial(exchange_kernel, shards),
        out_shape=(
            jax.ShapeDtypeStruct((2, shards, piece, 256), bf),
            halo,
            halo,
            jax.ShapeDtypeStruct((groups, rows, wide), bf),
            jax.ShapeDtypeStruct((groups, wide, wide), bf),
            jax.ShapeDtypeStruct((2, rows, 128), bf),
            jax.ShapeDtypeStruct((2, rows, 128), bf),
            jax.ShapeDtypeStruct((2,) + bands.shape, jnp.int32),
        ),
        in_specs=[ANY] * 6,
        out_specs=(ANY,) * 8,
        scratch_shapes=[
            pltpu.VMEM((groups, rows, wide), bf),
            pltpu.VMEM((wide, groups * wide), bf),
            pltpu.VMEM((2, rows, 128), bf),
        ]
        + [dma((shards,))] * 8
        + [dma((6,)), dma((groups,)), dma((groups,)), dma((6,)), dma((9,))],
        compiler_params=pltpu.CompilerParams(collective_id=0, has_side_effects=True),
        name="exchange",
    )(tk, tv, sq, cot, ow, bands)


def attend_kernel(
    tiles, shards, lo_ref, hi_ref, left, own, right, order, q_ref, g_ref, gp_ref, o_ref, dq_ref,
    arr, idx, hot, kv, kvt, s_scr, d_scr, p_scr, qb, gb, top_scr, stat_scr, sem,
):
    t = pl.program_id(0)
    f32 = jnp.float32
    bf = jnp.bfloat16
    L = 2 * F
    nb = F // SBLK
    per = CH // TBLK
    pad = kv.shape[0] - CH
    side = arr.shape[1]
    piece = side // shards
    irows = side // 128

    @pl.when(t == 0)
    def _():
        pair = lax.div(lax.axis_index("tm"), 2)
        copies = [
            pltpu.make_async_copy(left, arr.at[0], sem.at[0]),
            pltpu.make_async_copy(own.at[0], arr.at[1], sem.at[1]),
            pltpu.make_async_copy(own.at[1], arr.at[2], sem.at[2]),
            pltpu.make_async_copy(right, arr.at[3], sem.at[3]),
        ]
        for e in range(4):
            shard = lax.rem(2 * pair + shards - 1 + e, shards)
            at = pl.multiple_of(shard * irows, irows)
            copies.append(
                pltpu.make_async_copy(
                    order.at[pl.ds(at, irows)], idx.at[pl.ds(e * irows, irows)], sem.at[4 + e]
                )
            )
        for copy in copies:
            copy.start()
        kv[pad : pad + CH, :] = jnp.zeros((CH, 256), bf)
        kvt[:, pad : pad + CH] = jnp.zeros((256, CH), bf)
        for copy in copies:
            copy.wait()
        lane = lax.broadcasted_iota(jnp.int32, (128, 128), 1)

        def sort(j, carry):
            for r in range(GROUP // 128):
                row = idx[pl.ds(j * (GROUP // 128) + r, 1), :]
                col = jnp.broadcast_to(row, (128, 128)).T
                at = lax.div(col, side) * piece + lax.rem(col, piece)
                base = jnp.where(lax.rem(at, 128) == lane, lax.div(at, 128), -1)
                base = base.astype(f32).astype(bf)
                for k in range(side // 128):
                    hot[r * 128 : (r + 1) * 128, k * 128 : (k + 1) * 128] = jnp.where(
                        base == bf(k), bf(1), bf(0)
                    )
            e = lax.div(j * GROUP, side)
            rows = jnp.dot(hot[...], arr[e], preferred_element_type=f32)
            at = pl.multiple_of(j * GROUP, GROUP)
            kv[pl.ds(at, GROUP), :] = rows.astype(bf)
            kvt[:, pl.ds(at, GROUP)] = rows.T.astype(bf)
            return carry

        lax.fori_loop(0, pad // GROUP, sort, 0)

    def bounds(tile):
        los = [lo_ref[nb * tile + r] for r in range(nb)]
        his = [hi_ref[nb * tile + r] for r in range(nb)]
        low = functools.reduce(jnp.minimum, los)
        high = functools.reduce(jnp.maximum, his)
        return los, his, low, (high - low) // per + 1

    n = functools.reduce(jnp.maximum, [bounds(x)[3] for x in range(tiles)])
    lane = lax.broadcasted_iota(jnp.int32, (F, 128), 1)
    zero = jnp.zeros((F, 128), bf)
    nt = (((1,), (1,)), ((), ()))
    slot = lax.rem(t, 2)

    def start_at(first, k):
        return pl.multiple_of(jnp.minimum(first * TBLK + k * CH, pad), TBLK)

    def split_heads(x):
        return jnp.where(lane < HDIM, x, zero), jnp.where(lane < HDIM, zero, x)

    def join_heads(x):
        x = x.T
        return jnp.where(lane < HDIM, x[0:F], x[F:L])

    def step(do1, do2, do3):
        if do1:
            los, his, first1, _ = bounds(t)
            qb[0:F, :], qb[F:L, :] = split_heads(q_ref[...] * bf(1.0 / math.sqrt(HDIM)))
            gb[0:F, :], gb[F:L, :] = split_heads(g_ref[...])
            frame = lax.rem(lax.broadcasted_iota(jnp.int32, (8, L), 1), F) // SBLK
            lov = jnp.full((8, L), los[0], jnp.int32)
            hiv = jnp.full((8, L), his[0], jnp.int32)
            for r in range(1, nb):
                lov = jnp.where(frame == r, los[r], lov)
                hiv = jnp.where(frame == r, his[r], hiv)
        if do2:
            first2 = bounds(t - 1)[2]
            top2 = top_scr[...]
        if do3:
            first3 = bounds(t - 2)[2]
            delta = stat_scr[0]

        def body(k, carry):
            top, total, o, dq = carry
            at = pl.multiple_of(k * CH, CH)
            if do3:
                base = start_at(first3, k)
                e = p_scr[pl.ds(at, CH), :].astype(f32).reshape(CH // 8, 8, L)
                d = d_scr[slot, pl.ds(at, CH), :].reshape(CH // 8, 8, L)
                ds = (e * (d - delta[None])).reshape(CH, L).astype(bf)
                dq = dq + jnp.dot(kvt[0:128, pl.ds(base, CH)], ds, preferred_element_type=f32)
            if do2:
                base = start_at(first2, k)
                s = s_scr[pl.ds(at, CH), :].reshape(CH // 8, 8, L)
                e = jnp.exp(s - top2[None]).reshape(CH, L).astype(bf)
                p_scr[pl.ds(at, CH), :] = e
                total = total + jnp.sum(e.astype(f32).reshape(CH // 8, 8, L), axis=0)
                o = o + jnp.dot(kvt[128:256, pl.ds(base, CH)], e, preferred_element_type=f32)
            if do1:
                base = start_at(first1, k)
                s = lax.dot_general(
                    kv[pl.ds(base, CH), 0:128], qb[...], nt, preferred_element_type=f32
                )
                d_scr[slot, pl.ds(at, CH), :] = lax.dot_general(
                    kv[pl.ds(base, CH), 128:256], gb[...], nt, preferred_element_type=f32
                )
                for c in range(per):
                    block = first1 + k * per + c
                    ok = (block >= lov) & (block <= hiv)
                    bias = jnp.where(ok, 0.0, -jnp.inf).astype(f32)
                    part = s[c * 128 : (c + 1) * 128].reshape(16, 8, L) + bias[None]
                    s_scr[pl.ds(at + c * 128, 128), :] = part.reshape(128, L)
                    top = jnp.maximum(top, jnp.max(part, axis=0))
            return top, total, o, dq

        flat = jnp.zeros((8, L), f32)
        acc = jnp.zeros((128, L), f32)
        top, total, o, dq = lax.fori_loop(
            0, n, body, (jnp.full((8, L), -jnp.inf, f32), flat, acc, acc)
        )
        if do3:
            scale = stat_scr[1][0:1] * (1.0 / math.sqrt(HDIM))
            dq_ref[...] = join_heads(dq * scale).astype(bf)
        if do2:
            inv = 1.0 / jnp.sum(total, axis=0, keepdims=True)
            o = o * inv
            o_ref[...] = join_heads(o).astype(bf)
            grad = jnp.concatenate(split_heads(gp_ref[...]), axis=0).astype(f32).T
            stat_scr[0] = jnp.broadcast_to(jnp.sum(o * grad, axis=0, keepdims=True), (8, L))
            stat_scr[1] = jnp.broadcast_to(inv, (8, L))
        if do1:
            top_scr[...] = jnp.broadcast_to(jnp.max(top, axis=0, keepdims=True), (8, L))

    pl.when(t == 0)(lambda: step(True, False, False))
    pl.when(t == 1)(lambda: step(True, True, False))
    pl.when((t >= 2) & (t < tiles))(lambda: step(True, True, True))
    pl.when(t == tiles)(lambda: step(False, True, True))
    pl.when(t == tiles + 1)(lambda: step(False, False, True))


def attend(lo, hi, left, own, right, order, q, g, shards):
    frames = q.shape[0]
    side = left.shape[0]
    window = 4 * side
    reach = side // TBLK
    bf = jnp.bfloat16
    f32 = jnp.float32
    L = 2 * F
    tiles = frames // F
    keys = ((2 * reach + F // SBLK - 1) // (CH // TBLK) + 1) * CH
    now = lambda i, lo, hi: (jnp.minimum(i, tiles - 1), 0)
    one = lambda i, lo, hi: (jnp.clip(i - 1, 0, tiles - 1), 0)
    two = lambda i, lo, hi: (jnp.clip(i - 2, 0, tiles - 1), 0)
    return pl.pallas_call(
        functools.partial(attend_kernel, tiles, shards),
        grid_spec=pltpu.PrefetchScalarGridSpec(
            num_scalar_prefetch=2,
            grid=(tiles + 2,),
            in_specs=[ANY] * 4
            + [pl.BlockSpec((F, 128), now), pl.BlockSpec((F, 128), now), pl.BlockSpec((F, 128), one)],
            out_specs=(pl.BlockSpec((F, 128), one), pl.BlockSpec((F, 128), two)),
            scratch_shapes=[
                pltpu.VMEM((4, side, 256), bf),
                pltpu.VMEM((window // 128, 128), jnp.int32),
                pltpu.VMEM((GROUP, side), bf),
                pltpu.VMEM((window + CH, 256), bf),
                pltpu.VMEM((256, window + CH), bf),
                pltpu.VMEM((keys, L), f32),
                pltpu.VMEM((2, keys, L), f32),
                pltpu.VMEM((keys, L), bf),
                pltpu.VMEM((L, 128), bf),
                pltpu.VMEM((L, 128), bf),
                pltpu.VMEM((8, L), f32),
                pltpu.VMEM((2, 8, L), f32),
                pltpu.SemaphoreType.DMA((8,)),
            ],
        ),
        out_shape=(jax.ShapeDtypeStruct((frames, 128), bf),) * 2,
        name="attend",
    )(lo, hi, left, own, right, order, q, g, g)


def finish_kernel(
    shards, o_ref, dq_ref, cot, wcols, joined, dq, wsum,
    og, wg, got, red, ss, sr, gs, gr, ms, cs, ls,
):
    me = lax.axis_index("tm")
    c = lax.axis_index("clip")
    half = lax.rem(me, 2)
    mate = flip(me, 1)
    near, far = flip(c, 1), flip(c, 2)
    groups, rows, wide = og.shape
    bf = jnp.bfloat16
    f32 = jnp.float32
    part_rows, part_cols = red.shape
    greet(shards, (1, 2))

    own = pl.multiple_of(half * 128, 128)
    my_rows = pl.multiple_of(half * rows, 128)
    mate_rows = pl.multiple_of((1 - half) * rows, 128)
    o_mate = send(
        o_ref.at[pl.ds(mate_rows, rows)], og.at[c, :, pl.ds(own, 128)], (ms.at[0], ms.at[1]), tm=mate
    )
    dq_mate = send(
        dq_ref.at[pl.ds(mate_rows, rows)], dq.at[:, pl.ds(own, 128)], (ms.at[2], ms.at[3]), tm=mate
    )
    o_own = pltpu.make_async_copy(
        o_ref.at[pl.ds(my_rows, rows)], og.at[c, :, pl.ds(own, 128)], ls.at[0]
    )
    dq_own = pltpu.make_async_copy(
        dq_ref.at[pl.ds(my_rows, rows)], dq.at[:, pl.ds(own, 128)], ls.at[1]
    )
    o_far = send(og.at[c], og.at[c], (cs.at[0], cs.at[1]), clip=far)
    o_near = send(og.at[c], og.at[c], (cs.at[2], cs.at[3]), clip=near)
    o_relay = send(og.at[far], og.at[far], (cs.at[4], cs.at[5]), clip=near)

    def part_copy(d, src):
        target = lax.rem(me + d, shards)
        return send(
            wg.at[lax.div(target, 2), lax.rem(target, 2)], got.at[me],
            (ss.at[d], sr.at[src]), tm=target,
        )

    def place():
        at = pl.multiple_of(lax.div(me, 2) * part_rows, part_rows)
        col = pl.multiple_of(half * part_cols, 128)
        return wsum.at[pl.ds(at, part_rows), pl.ds(col, part_cols)]

    def sum_copy(d, src):
        return send(red, place(), (gs.at[d], gr.at[src]), tm=lax.rem(me + d, shards))

    o_mate.start()
    o_own.start()
    dq_mate.start()
    dq_own.start()
    o_own.wait()
    o_mate.wait()
    tn = (((0,), (0,)), ((), ()))
    block = og[c]
    for j in range(groups):
        part = lax.dot_general(block, cot[j], tn, preferred_element_type=f32).astype(bf)
        lanes = (j * wide) % part_cols
        wg[:, (j * wide) // part_cols, :, lanes : lanes + wide] = part.reshape(
            shards // 2, part_rows, wide
        )
    o_far.start()
    o_near.start()

    def start(d, carry):
        part_copy(d, me).start()
        return carry

    lax.fori_loop(1, shards, start, 0)
    got[pl.ds(me, 1)] = wg[lax.div(me, 2), pl.ds(half, 1)]
    o_far.wait_recv()
    o_relay.start()

    def arrive(d, carry):
        part_copy(d, lax.rem(me + shards - d, shards)).wait_recv()
        return carry

    lax.fori_loop(1, shards, arrive, 0)

    def add(s, acc):
        return acc + got[s].astype(f32)

    red[...] = lax.fori_loop(0, shards, add, jnp.zeros(red.shape, f32)).astype(bf)
    o_near.wait_recv()
    o_relay.wait_recv()

    def start_sum(d, carry):
        sum_copy(d, me).start()
        return carry

    lax.fori_loop(1, shards, start_sum, 0)
    put = pltpu.make_async_copy(red, place(), ls.at[2])
    put.start()
    total = jnp.zeros((rows, wide), f32)
    for j in range(groups):
        total += jnp.dot(og[j], wcols[j], preferred_element_type=f32)
    joined[...] = total.astype(bf)

    def end(d, carry):
        part_copy(d, lax.rem(me + shards - d, shards)).wait_send()
        sum_copy(d, lax.rem(me + shards - d, shards)).wait()
        return carry

    lax.fori_loop(1, shards, end, 0)
    put.wait()
    o_far.wait_send()
    o_near.wait_send()
    o_relay.wait_send()
    dq_mate.wait()
    dq_own.wait()


def finish(o, dq, cot, wcols, shards):
    bf = jnp.bfloat16
    dma = pltpu.SemaphoreType.DMA
    groups, rows, wide = cot.shape
    cols = groups * wide
    pr, pc = wide // (shards // 2), cols // 2
    vmem = pl.BlockSpec(memory_space=pltpu.VMEM)
    return pl.pallas_call(
        functools.partial(finish_kernel, shards),
        out_shape=(
            jax.ShapeDtypeStruct((rows, wide), bf),
            jax.ShapeDtypeStruct((rows, wide), bf),
            jax.ShapeDtypeStruct((wide, cols), bf),
        ),
        in_specs=[ANY, ANY, vmem, vmem],
        out_specs=(vmem, ANY, ANY),
        scratch_shapes=[
            pltpu.VMEM((groups, rows, wide), bf),
            pltpu.VMEM((shards // 2, 2, pr, pc), bf),
            pltpu.VMEM((shards, pr, pc), bf),
            pltpu.VMEM((pr, pc), bf),
            dma((shards,)), dma((shards,)), dma((shards,)), dma((shards,)),
            dma((4,)), dma((6,)), dma((3,)),
        ],
        compiler_params=pltpu.CompilerParams(collective_id=1, has_side_effects=True),
        name="finish",
    )(o, dq, cot, wcols)


def on_device(
    student_query,
    teacher_key,
    teacher_value,
    clip_order,
    band_start,
    band_end,
    output_weight,
    cotangent,
):
    shards = lax.axis_size("tm")
    groups = lax.axis_size("clip")
    pair = lax.axis_index("tm") // 2
    rows, wide = student_query.shape
    trows = teacher_key.shape[0]
    piece = trows // shards
    blocks = rows // SBLK

    bands = jnp.pad(jnp.stack([band_start, band_end]), ((0, 6), (0, 128 - blocks)))
    kv, left, right, cot_full, w_cols, q_pair, g_pair, b_pair = exchange(
        teacher_key.reshape(shards, piece, wide),
        teacher_value.reshape(shards, piece, wide),
        student_query, cotangent, output_weight, bands, shards, groups,
    )
    starts = b_pair[:, 0, :blocks].reshape(2 * blocks)
    ends = b_pair[:, 1, :blocks].reshape(2 * blocks)
    reach = trows // TBLK
    base = pair * 2 * blocks
    at = reach + jnp.arange(2 * blocks, dtype=jnp.int32)
    lo = jnp.maximum(at + starts, reach - base)
    hi = jnp.minimum(at + ends, shards * blocks - 1 + reach - base)

    o, dq = attend(
        lo, hi,
        left.reshape(trows, 256), kv.reshape(2, trows, 256), right.reshape(trows, 256),
        clip_order.reshape(-1, 128),
        q_pair.reshape(2 * rows, 128), g_pair.reshape(2 * rows, 128), shards,
    )
    joined, grad_query, wsum = finish(o, dq, cot_full, w_cols, shards)
    return (joined, grad_query, wsum.astype(jnp.float32))


def solution(mesh):
    return jax.shard_map(
        on_device,
        mesh=mesh,
        in_specs=(
            P("tm", "clip"),
            P("tm", "clip"),
            P("tm", "clip"),
            P(),
            P("tm"),
            P("tm"),
            P("clip", None),
            P("tm", "clip"),
        ),
        out_specs=(P("tm", "clip"), P("tm", "clip"), P("clip", None)),
        check_vma=False,
    )
```

```python
import functools
import math

import jax
import jax.numpy as jnp
from jax import lax
from jax.experimental import pallas as pl
from jax.experimental.pallas import tpu as pltpu
from jax.sharding import PartitionSpec as P

HDIM = 64
SBLK = 32
TBLK = 128
F = 128
CH = 1536
SUB = 512
GROUP = 1024
FAR = -3e38
ANY = pl.BlockSpec(memory_space=pl.ANY)
MESH = pl.DeviceIdType.MESH


def greet(shards, bits, wait=True):
    me = lax.axis_index("tm")
    c = lax.axis_index("clip")
    barrier = pltpu.get_barrier_semaphore()

    def tell(d, carry):
        pl.semaphore_signal(
            barrier, inc=1, device_id={"tm": lax.rem(me + d, shards)}, device_id_type=MESH
        )
        return carry

    lax.fori_loop(1, shards, tell, 0)
    for bit in bits:
        pl.semaphore_signal(
            barrier, inc=1, device_id={"clip": flip(c, bit)}, device_id_type=MESH
        )
    if wait:
        pl.semaphore_wait(barrier, shards - 1 + len(bits))


def flip(c, bit):
    if bit == 3:
        return 3 - c
    return c + bit - 2 * bit * lax.rem(lax.div(c, bit), 2)


def one_hot_rows(row, hot, at, side, piece):
    lane = lax.broadcasted_iota(jnp.int32, (128, 128), 1)
    col = jnp.broadcast_to(row, (128, 128)).T
    spot = lax.div(col, side) * piece + lax.rem(col, piece)
    base = jnp.where(lax.rem(spot, 128) == lane, lax.div(spot, 128), -1)
    base = base.astype(jnp.float32).astype(jnp.bfloat16)
    one = jnp.bfloat16(1)
    for k in range(side // 128):
        hot[at : at + 128, k * 128 : (k + 1) * 128] = jnp.maximum(
            one - jnp.abs(base - jnp.bfloat16(k)), jnp.bfloat16(0)
        )


def send(src, dst, sems, **where):
    return pltpu.make_async_remote_copy(
        src_ref=src, dst_ref=dst, send_sem=sems[0], recv_sem=sems[1],
        device_id=where, device_id_type=MESH,
    )


def step_kernel(
    shards, tiles, tk, tv, sq, cot, ow, starts, ends, order,
    joined, dq, wsum,
    kvin, left, right, idx, hot, kv, kvt, s0, s1, d0, d1, d2, p0, p1, qb, gb,
    cotv, wv, wcols, gv, qp, gp, bv, bp, band,
    o_send, dq_send, dq_own, og, wg, got, red,
    ks, kr, vs, vr, ls, lr, rs, rr, ss, sr, gs, gr,
    oss, osr, dss, dsr, ws, wr, cs, ms, fs, os_,
):
    f32 = jnp.float32
    bf = jnp.bfloat16
    me = lax.axis_index("tm")
    c = lax.axis_index("clip")
    half = lax.rem(me, 2)
    mate = flip(me, 1)
    pair = lax.div(me, 2)
    groups, rows_here, wide = cotv.shape
    near, far = flip(c, 1), flip(c, 2)
    prev = lax.rem(me + shards - 2, shards)
    after = lax.rem(me + 2, shards)
    L = 2 * F
    nb = F // SBLK
    per = CH // TBLK
    piece = tk.shape[1]
    side = shards * piece
    irows = side // 128
    blocks = F * tiles // SBLK
    half_blocks = blocks // 2
    half_tiles = tiles // 2
    reach = side // TBLK
    span = (2 * reach + nb) // per
    scores, dprobs, weights = (s0, s1), (d0, d1, d2), (p0, p1)
    part_rows, part_cols = red.shape
    own_cols = pl.ds(pl.multiple_of(half * 128, 128), 128)
    mate_cols = pl.ds(pl.multiple_of((1 - half) * 128, 128), 128)
    bv[...] = jnp.zeros_like(bv)
    bv[0:1, 0:half_blocks] = starts[...]
    bv[1:2, 0:half_blocks] = ends[...]
    greet(shards, (1, 2, 3))

    def key_copies(target, slot, src):
        p = lax.div(target, 2)
        col = pl.multiple_of(lax.rem(target, 2) * 128, 128)
        return (
            send(
                tk.at[pl.ds(2 * p, 2), :, pl.ds(col, 128)],
                kvin.at[:, me, :, pl.ds(0, 128)], (ks.at[slot], kr.at[src]), tm=target,
            ),
            send(
                tv.at[pl.ds(2 * p, 2), :, pl.ds(col, 128)],
                kvin.at[:, me, :, pl.ds(128, 128)], (vs.at[slot], vr.at[src]), tm=target,
            ),
        )

    def halo_copies(s):
        return (
            send(kvin.at[0, s], right.at[s], (rs.at[s], rr.at[s]), tm=prev),
            send(kvin.at[1, s], left.at[s], (ls.at[s], lr.at[s]), tm=after),
        )

    def w_copy(d, src):
        target = lax.rem(c + d, groups)
        theirs = pl.multiple_of(target * wide, 128)
        return send(
            ow.at[:, pl.ds(theirs, wide)], wcols.at[c], (ws.at[d], wr.at[src]), clip=target
        )

    mine = pl.multiple_of(c * wide, 128)
    cot_far = send(cot, cotv.at[c], (cs.at[0], cs.at[1]), clip=far)
    cot_near = send(cot, cotv.at[c], (cs.at[2], cs.at[3]), clip=near)
    cot_relay = send(cotv.at[far], cotv.at[far], (cs.at[4], cs.at[5]), clip=near)
    q_copy = send(sq.at[:, mate_cols], qp.at[half], (ms.at[0], ms.at[1]), tm=mate)
    b_copy = send(bv, bp.at[half], (ms.at[2], ms.at[3]), tm=mate)
    g_copy = send(gv.at[1 - half], gp.at[half], (ms.at[4], ms.at[5]), tm=mate)

    cot_far.start()
    cot_near.start()

    def start_keys(d, carry):
        for copy in key_copies(lax.rem(me + d, shards), d, me):
            copy.start()
        return carry

    lax.fori_loop(1, shards, start_keys, 0)
    q_copy.start()
    b_copy.start()
    mine_kv = (
        pltpu.make_async_copy(
            tk.at[pl.ds(2 * pair, 2), :, own_cols], kvin.at[:, me, :, pl.ds(0, 128)], os_.at[0]
        ),
        pltpu.make_async_copy(
            tv.at[pl.ds(2 * pair, 2), :, own_cols], kvin.at[:, me, :, pl.ds(128, 128)], os_.at[1]
        ),
    )
    mine_cot = (
        pltpu.make_async_copy(cot, cotv.at[c], os_.at[2]),
        pltpu.make_async_copy(ow, wv, os_.at[3]),
    )
    get_idx = []
    for e in range(4):
        at = pl.multiple_of(lax.rem(2 * pair + shards - 1 + e, shards) * irows, irows)
        get_idx.append(
            pltpu.make_async_copy(
                order.at[pl.ds(at, irows)], idx.at[pl.ds(e * irows, irows)], os_.at[7 + e]
            )
        )
    mine_rest = (
        pltpu.make_async_copy(ow.at[:, pl.ds(mine, wide)], wcols.at[c], os_.at[4]),
        pltpu.make_async_copy(sq.at[:, own_cols], qp.at[half], os_.at[5]),
        pltpu.make_async_copy(bv, bp.at[half], os_.at[6]),
    ) + tuple(get_idx)
    for copy in mine_cot + mine_kv + mine_rest:
        copy.start()
    for copy in mine_cot + mine_kv:
        copy.wait()
    for copy in halo_copies(me):
        copy.start()
    cot_far.wait_recv()
    cot_relay.start()
    cot_near.wait_recv()
    cot_relay.wait_recv()
    nt = (((1,), (1,)), ((), ()))
    grad = jnp.zeros((rows_here, wide), f32)
    for j in range(groups):
        grad += lax.dot_general(
            cotv[j], wv[:, j * wide : (j + 1) * wide], nt, preferred_element_type=f32
        )
    gv[0] = grad[:, 0:128].astype(bf)
    gv[1] = grad[:, 128:256].astype(bf)

    def forward(d, carry):
        s = lax.rem(me + shards - d, shards)
        for copy in key_copies(lax.rem(me + d, shards), d, s):
            copy.wait_recv()
        for copy in halo_copies(s):
            copy.start()
        return carry

    lax.fori_loop(1, 3, forward, 0)
    g_copy.start()
    put_g = pltpu.make_async_copy(gv.at[half], gp.at[half], os_.at[11])
    put_g.start()
    for copy in mine_rest:
        copy.wait()
    kvt[256:272, :] = jnp.ones((16, kvt.shape[1]), bf)
    lane = lax.broadcasted_iota(jnp.int32, (128, 128), 1)

    def mark(k, carry):
        at = pl.multiple_of(k * TBLK, TBLK)
        kv[pl.ds(at, TBLK), 128:256] = jnp.where(lane == k, 1.0, 0.0).astype(bf)
        return carry

    lax.fori_loop(0, 4 * reach, mark, 0)
    lax.fori_loop(3, shards, forward, 0)
    for d in range(1, groups):
        w_copy(d, c).start()

    def place(src, first, j):
        for r in range(GROUP // 128):
            row = lax.div(first, 128) + j * (GROUP // 128) + r
            one_hot_rows(idx[pl.ds(row, 1), :], hot, r * 128, side, piece)
        rows = jnp.dot(hot[...], src.reshape(side, 256), preferred_element_type=f32).astype(bf)
        at = pl.multiple_of(first + j * GROUP, GROUP)
        kv[pl.ds(at, GROUP), 0:128] = rows[:, 0:128]
        kv[pl.ds(at, GROUP), 256:384] = rows[:, 128:256]
        kvt[0:256, pl.ds(at, GROUP)] = rows.T

    def sort_own(j, carry):
        place(kvin[lax.div(j * GROUP, side)], side, j)
        return carry

    def sort_left(j, carry):
        place(left[...], 0, j)
        return carry

    def sort_right(j, carry):
        place(right[...], 3 * side, j)
        return carry

    lax.fori_loop(0, 2 * side // GROUP, sort_own, 0)
    q_copy.wait_recv()
    b_copy.wait_recv()
    g_copy.wait_recv()
    put_g.wait()
    get_band = pltpu.make_async_copy(bp, band, os_.at[12])
    get_band.start()
    get_band.wait()

    def came_left(s, carry):
        halo_copies(s)[1].wait_recv()
        return carry

    def came_right(s, carry):
        halo_copies(s)[0].wait_recv()
        return carry

    lax.fori_loop(0, shards, came_left, 0)
    lax.fori_loop(0, side // GROUP, sort_left, 0)
    lax.fori_loop(0, shards, came_right, 0)
    lax.fori_loop(0, side // GROUP, sort_right, 0)

    flane = lax.broadcasted_iota(jnp.int32, (F, 128), 1)
    zero = jnp.zeros((F, 128), bf)
    tops, deltas, invs = {}, {}, {}

    def tile_at(t):
        return lax.rem(t + (1 - half) * half_tiles, tiles)

    def frames(ref, t):
        at = pl.multiple_of(lax.rem(tile_at(t), half_tiles) * F, F)
        return ref[lax.div(tile_at(t), half_tiles), pl.ds(at, F), :]

    def split_heads(x):
        return jnp.where(flane < HDIM, x, zero), jnp.where(flane < HDIM, zero, x)

    def join_heads(x):
        x = x.T
        return jnp.where(flane < HDIM, x[0:F], x[F:L])

    def spot(t, k, u):
        return pl.multiple_of(tile_at(t) * (nb * TBLK) + k * CH + u * SUB, TBLK)

    def o_copy(t):
        part = pl.ds(t * F, F)
        return send(
            o_send.at[part], og.at[c, part, own_cols], (oss.at[t], osr.at[t]), tm=mate
        )

    def dq_copy(t):
        part = pl.ds(t * F, F)
        return send(
            dq_send.at[part], dq.at[part, own_cols], (dss.at[t], dsr.at[t]), tm=mate
        )

    for t in range(tiles + 2):
        do1, do2, do3 = t < tiles, 1 <= t <= tiles, t >= 2
        if do1:
            q = frames(qp, t) * bf(1.0 / math.sqrt(HDIM))
            qb[0:F, 0:128], qb[F:L, 0:128] = split_heads(q)
            gb[0:F, :], gb[F:L, :] = split_heads(frames(gp, t))
            block = lax.broadcasted_iota(jnp.int32, (SBLK, 128), 1)
            row = lax.div(tile_at(t), half_tiles)
            col = lax.rem(tile_at(t), half_tiles) * nb
            base_block = pair * blocks
            for r in range(nb):
                at = reach + tile_at(t) * nb + r
                lo = jnp.maximum(at + band[row, 0, col + r], reach - base_block)
                hi = jnp.minimum(
                    at + band[row, 1, col + r], shards * half_blocks - 1 + reach - base_block
                )
                bias = jnp.where((block >= lo) & (block <= hi), 0.0, FAR).astype(bf)
                qb[r * SBLK : (r + 1) * SBLK, 128:256] = bias
                qb[F + r * SBLK : F + (r + 1) * SBLK, 128:256] = bias

        def body(k, carry):
            top, o, dqt = carry
            for u in range(CH // SUB):
                at = pl.multiple_of(k * CH + u * SUB, SUB)
                if do1:
                    base = spot(t, k, u)
                    s = lax.dot_general(
                        kv[pl.ds(base, SUB), 0:256], qb[...], nt, preferred_element_type=f32
                    )
                    dprobs[t % 3][pl.ds(at, SUB), :] = lax.dot_general(
                        kv[pl.ds(base, SUB), 256:384], gb[...], nt, preferred_element_type=f32
                    )
                    scores[t % 2][pl.ds(at, SUB), :] = s
                    top = jnp.maximum(top, jnp.max(s.reshape(SUB // 8, 8, L), axis=0))
                if do2:
                    base = spot(t - 1, k, u)
                    s = scores[(t - 1) % 2][pl.ds(at, SUB), :].reshape(SUB // 8, 8, L)
                    e = jnp.exp(s - tops[t - 1][None]).reshape(SUB, L).astype(bf)
                    weights[(t - 1) % 2][pl.ds(at, SUB), :] = e
                    o = o + jnp.dot(kvt[128:272, pl.ds(base, SUB)], e, preferred_element_type=f32)
                if do3:
                    base = spot(t - 2, k, u)
                    e = weights[t % 2][pl.ds(at, SUB), :].astype(f32).reshape(SUB // 8, 8, L)
                    d = dprobs[(t - 2) % 3][pl.ds(at, SUB), :].reshape(SUB // 8, 8, L)
                    ds = (e * (d - deltas[t - 2][None])).reshape(SUB, L).astype(bf)
                    dqt = dqt + jnp.dot(
                        kvt[0:128, pl.ds(base, SUB)], ds, preferred_element_type=f32
                    )
            return top, o, dqt

        top, o, dqt = lax.fori_loop(
            0, span, body,
            (
                jnp.full((8, L), -jnp.inf, f32),
                jnp.zeros((144, L), f32),
                jnp.zeros((128, L), f32),
            ),
        )
        if 2 <= t < half_tiles + 2:
            o_copy(t - 2).start()
        if 3 <= t < half_tiles + 3:
            dq_copy(t - 3).start()
        if do3:
            scale = invs[t - 2] * (1.0 / math.sqrt(HDIM))
            out = join_heads(dqt * scale).astype(bf)
            if t - 2 < half_tiles:
                dq_send[(t - 2) * F : (t - 1) * F, :] = out
            else:
                dq_own[(t - 2 - half_tiles) * F : (t - 1 - half_tiles) * F, :] = out
        if do2:
            inv = 1.0 / o[128:129]
            o = o[0:128] * inv
            out = join_heads(o).astype(bf)
            if t - 1 < half_tiles:
                o_send[(t - 1) * F : t * F, :] = out
            else:
                og[c, (t - 1 - half_tiles) * F : (t - half_tiles) * F, own_cols] = out
            grad = jnp.concatenate(split_heads(frames(gp, t - 1)), axis=0).astype(f32).T
            deltas[t - 1] = jnp.broadcast_to(jnp.sum(o * grad, axis=0, keepdims=True), (8, L))
            invs[t - 1] = inv
        if do1:
            tops[t] = jnp.broadcast_to(jnp.max(top, axis=0, keepdims=True), (8, L))

    o_far = send(og.at[c], og.at[c], (fs.at[0], fs.at[1]), clip=far)
    o_near = send(og.at[c], og.at[c], (fs.at[2], fs.at[3]), clip=near)
    o_relay = send(og.at[far], og.at[far], (fs.at[4], fs.at[5]), clip=near)
    put_dq = pltpu.make_async_copy(dq_own, dq.at[:, own_cols], os_.at[13])

    def ahead(d):
        return lax.rem(me + lax.rem(13 * d, shards), shards)

    def behind(d):
        return lax.rem(me + shards - lax.rem(13 * d, shards), shards)

    def part_copy(d, src):
        target = ahead(d)
        return send(
            wg.at[lax.div(target, 2), lax.rem(target, 2)], got.at[me],
            (ss.at[d], sr.at[src]), tm=target,
        )

    def spot_of_sum():
        at = pl.multiple_of(lax.div(me, 2) * part_rows, part_rows)
        col = pl.multiple_of(half * part_cols, 128)
        return wsum.at[pl.ds(at, part_rows), pl.ds(col, part_cols)]

    def sum_copy(d, src):
        return send(red, spot_of_sum(), (gs.at[d], gr.at[src]), tm=ahead(d))

    for t in range(half_tiles):
        o_copy(t).wait_recv()
    turned = og[c].T
    for j in range(groups):
        part = jnp.dot(turned, cotv[j], preferred_element_type=f32).astype(bf)
        lanes = (j * wide) % part_cols
        wg[:, (j * wide) // part_cols, :, lanes : lanes + wide] = part.reshape(
            shards // 2, part_rows, wide
        )
    put_dq.start()

    def start(d, carry):
        part_copy(d, me).start()
        return carry

    lax.fori_loop(1, shards, start, 0)
    o_far.start()
    o_near.start()
    got[pl.ds(me, 1)] = wg[lax.div(me, 2), pl.ds(half, 1)]

    def arrive(d, carry):
        part_copy(d, behind(d)).wait_recv()
        return carry

    lax.fori_loop(1, shards, arrive, 0)

    def add(s, acc):
        return acc + got[s].astype(f32)

    red[...] = lax.fori_loop(0, shards, add, jnp.zeros(red.shape, f32)).astype(bf)
    o_far.wait_recv()
    o_relay.start()

    def start_sum(d, carry):
        sum_copy(d, me).start()
        return carry

    lax.fori_loop(1, shards, start_sum, 0)
    put = pltpu.make_async_copy(red, spot_of_sum(), os_.at[14])
    put.start()
    o_near.wait_recv()
    o_relay.wait_recv()
    for d in range(1, groups):
        w_copy(d, lax.rem(c + groups - d, groups)).wait()
    total = jnp.zeros((rows_here, wide), f32)
    for j in range(groups):
        total += jnp.dot(og[j], wcols[j], preferred_element_type=f32)
    joined[...] = total.astype(bf)
    for t in range(half_tiles):
        o_copy(t).wait_send()
        dq_copy(t).wait()

    def end(d, carry):
        part_copy(d, behind(d)).wait_send()
        sum_copy(d, behind(d)).wait()
        return carry

    lax.fori_loop(1, shards, end, 0)
    put.wait()
    put_dq.wait()
    o_far.wait_send()
    o_near.wait_send()
    o_relay.wait_send()
    cot_far.wait_send()
    cot_near.wait_send()
    cot_relay.wait_send()
    q_copy.wait_send()
    b_copy.wait_send()
    g_copy.wait_send()

    def drain(d, carry):
        for copy in key_copies(lax.rem(me + d, shards), d, me):
            copy.wait_send()
        return carry

    def drain_halos(s, carry):
        for copy in halo_copies(s):
            copy.wait_send()
        return carry

    lax.fori_loop(1, shards, drain, 0)
    lax.fori_loop(0, shards, drain_halos, 0)


def step(tk, tv, sq, cot, ow, starts, ends, order, shards, groups):
    bf = jnp.bfloat16
    f32 = jnp.float32
    rows, wide = sq.shape
    piece = tk.shape[1]
    side = shards * piece
    window = 4 * side
    reach = side // TBLK
    L = 2 * F
    tiles = 2 * rows // F
    keys = (2 * reach + F // SBLK) * TBLK
    cols = groups * wide
    pr, pc = wide // (shards // 2), cols // 2
    dma = pltpu.SemaphoreType.DMA
    vmem = pl.BlockSpec(memory_space=pltpu.VMEM)
    return pl.pallas_call(
        functools.partial(step_kernel, shards, tiles),
        out_shape=(
            jax.ShapeDtypeStruct((rows, wide), bf),
            jax.ShapeDtypeStruct((rows, wide), bf),
            jax.ShapeDtypeStruct((wide, cols), bf),
        ),
        in_specs=[ANY] * 5 + [vmem] * 2 + [ANY],
        out_specs=(vmem, ANY, ANY),
        scratch_shapes=[
            pltpu.VMEM((2, shards, piece, 256), bf),
            pltpu.VMEM((shards, piece, 256), bf),
            pltpu.VMEM((shards, piece, 256), bf),
            pltpu.VMEM((window // 128, 128), jnp.int32),
            pltpu.VMEM((GROUP, side), bf),
            pltpu.VMEM((window, 384), bf),
            pltpu.VMEM((272, window), bf),
        ]
        + [pltpu.VMEM((keys, L), f32)] * 5
        + [pltpu.VMEM((keys, L), bf)] * 2
        + [
            pltpu.VMEM((L, 256), bf),
            pltpu.VMEM((L, 128), bf),
            pltpu.VMEM((groups, rows, wide), bf),
            pltpu.VMEM((wide, cols), bf),
            pltpu.VMEM((groups, wide, wide), bf),
            pltpu.VMEM((2, rows, 128), bf),
            pltpu.VMEM((2, rows, 128), bf),
            pltpu.VMEM((2, rows, 128), bf),
            pltpu.VMEM((8, 128), jnp.int32),
            pltpu.VMEM((2, 8, 128), jnp.int32),
            pltpu.SMEM((2, 8, 128), jnp.int32),
            pltpu.VMEM((rows, 128), bf),
            pltpu.VMEM((rows, 128), bf),
            pltpu.VMEM((rows, 128), bf),
            pltpu.VMEM((groups, rows, wide), bf),
            pltpu.VMEM((shards // 2, 2, pr, pc), bf),
            pltpu.VMEM((shards, pr, pc), bf),
            pltpu.VMEM((pr, pc), bf),
        ]
        + [dma((shards,))] * 12
        + [dma((tiles // 2,))] * 4
        + [dma((groups,))] * 2
        + [dma((6,))] * 3
        + [dma((15,))],
        compiler_params=pltpu.CompilerParams(
            collective_id=0, has_side_effects=True, vmem_limit_bytes=67043328
        ),
        name="step",
    )(tk, tv, sq, cot, ow, starts, ends, order)


def settle_kernel(joined, dq, wsum, joined_out, dq_out, w_out):
    joined_out[...] = joined[...]
    dq_out[...] = dq[...]
    w_out[...] = wsum[...].astype(jnp.float32)


def settle(joined, dq, wsum):
    steps = 2
    arrays = (joined, dq, wsum)
    specs = [
        pl.BlockSpec((x.shape[0] // steps, x.shape[1]), lambda i: (i, 0)) for x in arrays
    ]
    return pl.pallas_call(
        settle_kernel,
        grid=(steps,),
        in_specs=specs,
        out_specs=tuple(specs),
        out_shape=(
            jax.ShapeDtypeStruct(joined.shape, joined.dtype),
            jax.ShapeDtypeStruct(dq.shape, dq.dtype),
            jax.ShapeDtypeStruct(wsum.shape, jnp.float32),
        ),
        name="settle",
    )(joined, dq, wsum)


def on_device(
    student_query,
    teacher_key,
    teacher_value,
    clip_order,
    band_start,
    band_end,
    output_weight,
    cotangent,
):
    shards = lax.axis_size("tm")
    groups = lax.axis_size("clip")
    rows, wide = student_query.shape
    trows = teacher_key.shape[0]
    piece = trows // shards
    blocks = rows // SBLK

    return settle(
        *step(
            teacher_key.reshape(shards, piece, wide),
            teacher_value.reshape(shards, piece, wide),
            student_query, cotangent, output_weight,
            band_start.reshape(1, blocks), band_end.reshape(1, blocks),
            clip_order.reshape(-1, 128), shards, groups,
        )
    )


def solution(mesh):
    return jax.shard_map(
        on_device,
        mesh=mesh,
        in_specs=(
            P("tm", "clip"),
            P("tm", "clip"),
            P("tm", "clip"),
            P(),
            P("tm"),
            P("tm"),
            P("clip", None),
            P("tm", "clip"),
        ),
        out_specs=(P("tm", "clip"), P("tm", "clip"), P("clip", None)),
        check_vma=False,
    )
```

```python
import functools
import math

import jax
import jax.numpy as jnp
from jax import lax
from jax.experimental import pallas as pl
from jax.experimental.pallas import tpu as pltpu
from jax.sharding import PartitionSpec as P

HDIM = 64
SBLK = 32
TBLK = 128
F = 128
CH = 1536
SUB = 512
GROUP = 1024
FAR = -3e38
ANY = pl.BlockSpec(memory_space=pl.ANY)
MESH = pl.DeviceIdType.MESH


def greet(shards, bits, wait=True):
    me = lax.axis_index("tm")
    c = lax.axis_index("clip")
    barrier = pltpu.get_barrier_semaphore()

    def tell(d, carry):
        pl.semaphore_signal(
            barrier, inc=1, device_id={"tm": lax.rem(me + d, shards)}, device_id_type=MESH
        )
        return carry

    lax.fori_loop(1, shards, tell, 0)
    for bit in bits:
        pl.semaphore_signal(
            barrier, inc=1, device_id={"clip": flip(c, bit)}, device_id_type=MESH
        )
    if wait:
        pl.semaphore_wait(barrier, shards - 1 + len(bits))


def flip(c, bit):
    if bit == 3:
        return 3 - c
    return c + bit - 2 * bit * lax.rem(lax.div(c, bit), 2)


def one_hot_rows(row, hot, at, side, piece):
    lane = lax.broadcasted_iota(jnp.int32, (128, 128), 1)
    col = jnp.broadcast_to(row, (128, 128)).T
    spot = lax.div(col, side) * piece + lax.rem(col, piece)
    base = jnp.where(lax.rem(spot, 128) == lane, lax.div(spot, 128), -1)
    base = base.astype(jnp.float32).astype(jnp.bfloat16)
    one = jnp.bfloat16(1)
    for k in range(side // 128):
        hot[at : at + 128, k * 128 : (k + 1) * 128] = jnp.maximum(
            one - jnp.abs(base - jnp.bfloat16(k)), jnp.bfloat16(0)
        )


def send(src, dst, sems, **where):
    return pltpu.make_async_remote_copy(
        src_ref=src, dst_ref=dst, send_sem=sems[0], recv_sem=sems[1],
        device_id=where, device_id_type=MESH,
    )


def step_kernel(
    shards, tiles, tk, tv, sq, cot, ow, starts, ends, order,
    joined, dq, wsum,
    kvin, left, right, idx, hot, kv, kvt, s0, s1, d0, d1, d2, p0, p1, p2, p3, p4, p5, qb, gb, gb2,
    cotv, wv, wcols, gv, qp, gp, bv, bp, band,
    o_send, dq_send, dq_own, og, wg, got, red,
    ks, kr, vs, vr, ls, lr, rs, rr, ss, sr, gs, gr,
    oss, osr, dss, dsr, ws, wr, cs, ms, fs, os_,
):
    f32 = jnp.float32
    bf = jnp.bfloat16
    me = lax.axis_index("tm")
    c = lax.axis_index("clip")
    half = lax.rem(me, 2)
    mate = flip(me, 1)
    pair = lax.div(me, 2)
    groups, rows_here, wide = cotv.shape
    near, far = flip(c, 1), flip(c, 2)
    prev = lax.rem(me + shards - 2, shards)
    after = lax.rem(me + 2, shards)
    L = 2 * F
    nb = F // SBLK
    per = CH // TBLK
    piece = tk.shape[1]
    side = shards * piece
    irows = side // 128
    blocks = F * tiles // SBLK
    half_blocks = blocks // 2
    half_tiles = tiles // 2
    reach = side // TBLK
    span = (2 * reach + nb) // per
    scores, dprobs = (s0, s1), (d0, d1, d2)
    part_rows, part_cols = red.shape
    own_cols = pl.ds(pl.multiple_of(half * 128, 128), 128)
    mate_cols = pl.ds(pl.multiple_of((1 - half) * 128, 128), 128)
    bv[...] = jnp.zeros_like(bv)
    bv[0:1, 0:half_blocks] = starts[...]
    bv[1:2, 0:half_blocks] = ends[...]
    greet(shards, (1, 2, 3))

    def key_copies(target, slot, src):
        p = lax.div(target, 2)
        col = pl.multiple_of(lax.rem(target, 2) * 128, 128)
        return (
            send(
                tk.at[pl.ds(2 * p, 2), :, pl.ds(col, 128)],
                kvin.at[:, me, :, pl.ds(0, 128)], (ks.at[slot], kr.at[src]), tm=target,
            ),
            send(
                tv.at[pl.ds(2 * p, 2), :, pl.ds(col, 128)],
                kvin.at[:, me, :, pl.ds(128, 128)], (vs.at[slot], vr.at[src]), tm=target,
            ),
        )

    def halo_copies(s):
        return (
            send(kvin.at[0, s], right.at[s], (rs.at[s], rr.at[s]), tm=prev),
            send(kvin.at[1, s], left.at[s], (ls.at[s], lr.at[s]), tm=after),
        )

    def w_copy(d, src):
        target = lax.rem(c + d, groups)
        theirs = pl.multiple_of(target * wide, 128)
        return send(
            ow.at[:, pl.ds(theirs, wide)], wcols.at[c], (ws.at[d], wr.at[src]), clip=target
        )

    mine = pl.multiple_of(c * wide, 128)
    cot_far = send(cot, cotv.at[c], (cs.at[0], cs.at[1]), clip=far)
    cot_near = send(cot, cotv.at[c], (cs.at[2], cs.at[3]), clip=near)
    cot_relay = send(cotv.at[far], cotv.at[far], (cs.at[4], cs.at[5]), clip=near)
    q_copy = send(sq.at[:, mate_cols], qp.at[half], (ms.at[0], ms.at[1]), tm=mate)
    b_copy = send(bv, bp.at[half], (ms.at[2], ms.at[3]), tm=mate)
    g_copy = send(gv.at[1 - half], gp.at[half], (ms.at[4], ms.at[5]), tm=mate)

    cot_far.start()
    cot_near.start()

    def start_keys(d, carry):
        for copy in key_copies(lax.rem(me + d, shards), d, me):
            copy.start()
        return carry

    lax.fori_loop(1, shards, start_keys, 0)
    q_copy.start()
    b_copy.start()
    mine_kv = (
        pltpu.make_async_copy(
            tk.at[pl.ds(2 * pair, 2), :, own_cols], kvin.at[:, me, :, pl.ds(0, 128)], os_.at[0]
        ),
        pltpu.make_async_copy(
            tv.at[pl.ds(2 * pair, 2), :, own_cols], kvin.at[:, me, :, pl.ds(128, 128)], os_.at[1]
        ),
    )
    mine_cot = (
        pltpu.make_async_copy(cot, cotv.at[c], os_.at[2]),
        pltpu.make_async_copy(ow, wv, os_.at[3]),
    )
    get_idx = []
    for e in range(4):
        at = pl.multiple_of(lax.rem(2 * pair + shards - 1 + e, shards) * irows, irows)
        get_idx.append(
            pltpu.make_async_copy(
                order.at[pl.ds(at, irows)], idx.at[pl.ds(e * irows, irows)], os_.at[7 + e]
            )
        )
    mine_rest = (
        pltpu.make_async_copy(ow.at[:, pl.ds(mine, wide)], wcols.at[c], os_.at[4]),
        pltpu.make_async_copy(sq.at[:, own_cols], qp.at[half], os_.at[5]),
        pltpu.make_async_copy(bv, bp.at[half], os_.at[6]),
    ) + tuple(get_idx)
    for copy in mine_cot + mine_kv + mine_rest:
        copy.start()
    for copy in mine_cot + mine_kv:
        copy.wait()
    for copy in halo_copies(me):
        copy.start()
    cot_far.wait_recv()
    cot_relay.start()
    cot_near.wait_recv()
    cot_relay.wait_recv()
    nt = (((1,), (1,)), ((), ()))
    grad = jnp.zeros((rows_here, wide), f32)
    for j in range(groups):
        grad += lax.dot_general(
            cotv[j], wv[:, j * wide : (j + 1) * wide], nt, preferred_element_type=f32
        )
    gv[0] = grad[:, 0:128].astype(bf)
    gv[1] = grad[:, 128:256].astype(bf)

    def forward(d, carry):
        s = lax.rem(me + shards - d, shards)
        for copy in key_copies(lax.rem(me + d, shards), d, s):
            copy.wait_recv()
        for copy in halo_copies(s):
            copy.start()
        return carry

    lax.fori_loop(1, 3, forward, 0)
    g_copy.start()
    put_g = pltpu.make_async_copy(gv.at[half], gp.at[half], os_.at[11])
    put_g.start()
    for copy in mine_rest:
        copy.wait()
    kvt[256:272, :] = jnp.ones((16, kvt.shape[1]), bf)
    lane = lax.broadcasted_iota(jnp.int32, (128, 128), 1)

    def mark(k, carry):
        at = pl.multiple_of(k * TBLK, TBLK)
        kv[pl.ds(at, TBLK), 128:256] = jnp.where(lane == k, 1.0, 0.0).astype(bf)
        return carry

    lax.fori_loop(0, 4 * reach, mark, 0)
    lax.fori_loop(3, shards, forward, 0)
    for d in range(1, groups):
        w_copy(d, c).start()

    def place(src, first, j):
        for r in range(GROUP // 128):
            row = lax.div(first, 128) + j * (GROUP // 128) + r
            one_hot_rows(idx[pl.ds(row, 1), :], hot, r * 128, side, piece)
        rows = jnp.dot(hot[...], src.reshape(side, 256), preferred_element_type=f32).astype(bf)
        at = pl.multiple_of(first + j * GROUP, GROUP)
        kv[pl.ds(at, GROUP), 0:128] = rows[:, 0:128]
        kv[pl.ds(at, GROUP), 256:384] = rows[:, 128:256]
        kvt[0:256, pl.ds(at, GROUP)] = rows.T

    def sort_own(j, carry):
        place(kvin[lax.div(j * GROUP, side)], side, j)
        return carry

    def sort_left(j, carry):
        place(left[...], 0, j)
        return carry

    def sort_right(j, carry):
        place(right[...], 3 * side, j)
        return carry

    lax.fori_loop(0, 2 * side // GROUP, sort_own, 0)
    q_copy.wait_recv()
    b_copy.wait_recv()
    g_copy.wait_recv()
    put_g.wait()
    get_band = pltpu.make_async_copy(bp, band, os_.at[12])
    get_band.start()
    get_band.wait()

    def came_left(s, carry):
        halo_copies(s)[1].wait_recv()
        return carry

    def came_right(s, carry):
        halo_copies(s)[0].wait_recv()
        return carry

    lax.fori_loop(0, shards, came_left, 0)
    lax.fori_loop(0, side // GROUP, sort_left, 0)
    lax.fori_loop(0, shards, came_right, 0)
    lax.fori_loop(0, side // GROUP, sort_right, 0)

    flane = lax.broadcasted_iota(jnp.int32, (F, 128), 1)
    zero = jnp.zeros((F, 128), bf)
    tops, deltas, invs = {}, {}, {}
    scale = 1.0 / math.sqrt(HDIM)

    def weights(t):
        return (p0, p1)[t % 2] if t < half_tiles else (p2, p3, p4, p5)[t - half_tiles]

    def tile_at(t):
        return lax.rem(t + (1 - half) * half_tiles, tiles)

    def frames(ref, t):
        at = pl.multiple_of(lax.rem(tile_at(t), half_tiles) * F, F)
        return ref[lax.div(tile_at(t), half_tiles), pl.ds(at, F), :]

    def split_heads(x):
        return jnp.where(flane < HDIM, x, zero), jnp.where(flane < HDIM, zero, x)

    def join_heads(x):
        x = x.T
        return jnp.where(flane < HDIM, x[0:F], x[F:L])

    def spot(t, k, u):
        return pl.multiple_of(tile_at(t) * (nb * TBLK) + k * CH + u * SUB, TBLK)

    def o_copy(t):
        part = pl.ds(t * F, F)
        return send(
            o_send.at[part], og.at[c, part, own_cols], (oss.at[t], osr.at[t]), tm=mate
        )

    def dq_copy(t):
        part = pl.ds(t * F, F)
        return send(
            dq_send.at[part], dq.at[part, own_cols], (dss.at[t], dsr.at[t]), tm=mate
        )

    for t in range(tiles + 1):
        do1, do2, do3 = t < tiles, t >= 1, 2 <= t < half_tiles + 2
        keep = t < half_tiles
        if do1:
            q = frames(qp, t) * bf(1.0 / math.sqrt(HDIM))
            qb[0:F, 0:128], qb[F:L, 0:128] = split_heads(q)
            if keep:
                gb[0:F, :], gb[F:L, :] = split_heads(frames(gp, t))
            block = lax.broadcasted_iota(jnp.int32, (SBLK, 128), 1)
            row = lax.div(tile_at(t), half_tiles)
            col = lax.rem(tile_at(t), half_tiles) * nb
            base_block = pair * blocks
            for r in range(nb):
                at = reach + tile_at(t) * nb + r
                lo = jnp.maximum(at + band[row, 0, col + r], reach - base_block)
                hi = jnp.minimum(
                    at + band[row, 1, col + r], shards * half_blocks - 1 + reach - base_block
                )
                bias = jnp.where((block >= lo) & (block <= hi), 0.0, FAR).astype(bf)
                qb[r * SBLK : (r + 1) * SBLK, 128:256] = bias
                qb[F + r * SBLK : F + (r + 1) * SBLK, 128:256] = bias

        def body(k, carry):
            top, o, dqt = carry
            for u in range(CH // SUB):
                at = pl.multiple_of(k * CH + u * SUB, SUB)
                if do1:
                    base = spot(t, k, u)
                    s = lax.dot_general(
                        kv[pl.ds(base, SUB), 0:256], qb[...], nt, preferred_element_type=f32
                    )
                    if keep:
                        dprobs[t % 3][pl.ds(at, SUB), :] = lax.dot_general(
                            kv[pl.ds(base, SUB), 256:384], gb[...], nt, preferred_element_type=f32
                        )
                    scores[t % 2][pl.ds(at, SUB), :] = s
                    top = jnp.maximum(top, jnp.max(s.reshape(SUB // 8, 8, L), axis=0))
                if do2:
                    base = spot(t - 1, k, u)
                    s = scores[(t - 1) % 2][pl.ds(at, SUB), :].reshape(SUB // 8, 8, L)
                    e = jnp.exp(s - tops[t - 1][None]).reshape(SUB, L).astype(bf)
                    weights(t - 1)[pl.ds(at, SUB), :] = e
                    o = o + jnp.dot(kvt[128:272, pl.ds(base, SUB)], e, preferred_element_type=f32)
                if do3:
                    base = spot(t - 2, k, u)
                    e = weights(t - 2)[pl.ds(at, SUB), :].astype(f32).reshape(SUB // 8, 8, L)
                    d = dprobs[(t - 2) % 3][pl.ds(at, SUB), :].reshape(SUB // 8, 8, L)
                    ds = (e * (d - deltas[t - 2][None])).reshape(SUB, L).astype(bf)
                    dqt = dqt + jnp.dot(
                        kvt[0:128, pl.ds(base, SUB)], ds, preferred_element_type=f32
                    )
            return top, o, dqt

        top, o, dqt = lax.fori_loop(
            0, span, body,
            (
                jnp.full((8, L), -jnp.inf, f32),
                jnp.zeros((144, L), f32),
                jnp.zeros((128, L), f32),
            ),
        )
        if 2 <= t < half_tiles + 2:
            o_copy(t - 2).start()
        if 3 <= t < half_tiles + 3:
            dq_copy(t - 3).start()
        if do3:
            out = join_heads(dqt * (invs[t - 2] * scale)).astype(bf)
            dq_send[(t - 2) * F : (t - 1) * F, :] = out
        if do2:
            inv = 1.0 / o[128:129]
            o = o[0:128] * inv
            out = join_heads(o).astype(bf)
            if t - 1 < half_tiles:
                o_send[(t - 1) * F : t * F, :] = out
            else:
                og[c, (t - 1 - half_tiles) * F : (t - half_tiles) * F, own_cols] = out
            grad = jnp.concatenate(split_heads(frames(gp, t - 1)), axis=0).astype(f32).T
            deltas[t - 1] = jnp.broadcast_to(jnp.sum(o * grad, axis=0, keepdims=True), (8, L))
            invs[t - 1] = inv
        if do1:
            tops[t] = jnp.broadcast_to(jnp.max(top, axis=0, keepdims=True), (8, L))

    def leave(first):
        pairs = ((first, gb), (first + 1, gb2))
        for t, ref in pairs:
            ref[0:F, :], ref[F:L, :] = split_heads(frames(gp, t))

        def body(k, carry):
            carry = list(carry)
            for u in range(CH // SUB):
                at = pl.multiple_of(k * CH + u * SUB, SUB)
                for i, (t, ref) in enumerate(pairs):
                    base = spot(t, k, u)
                    d = lax.dot_general(
                        kv[pl.ds(base, SUB), 256:384], ref[...], nt, preferred_element_type=f32
                    ).reshape(SUB // 8, 8, L)
                    e = weights(t)[pl.ds(at, SUB), :].astype(f32).reshape(SUB // 8, 8, L)
                    ds = (e * (d - deltas[t][None])).reshape(SUB, L).astype(bf)
                    carry[i] = carry[i] + jnp.dot(
                        kvt[0:128, pl.ds(base, SUB)], ds, preferred_element_type=f32
                    )
            return tuple(carry)

        sums = lax.fori_loop(0, span, body, (jnp.zeros((128, L), f32),) * 2)
        for (t, _), dqt in zip(pairs, sums):
            at = (t - half_tiles) * F
            dq_own[at : at + F, :] = join_heads(dqt * (invs[t] * scale)).astype(bf)

    o_far = send(og.at[c], og.at[c], (fs.at[0], fs.at[1]), clip=far)
    o_near = send(og.at[c], og.at[c], (fs.at[2], fs.at[3]), clip=near)
    o_relay = send(og.at[far], og.at[far], (fs.at[4], fs.at[5]), clip=near)
    put_dq = pltpu.make_async_copy(dq_own, dq.at[:, own_cols], os_.at[13])

    def ahead(d):
        return lax.rem(me + lax.rem(13 * d, shards), shards)

    def behind(d):
        return lax.rem(me + shards - lax.rem(13 * d, shards), shards)

    def part_copy(d, src):
        target = ahead(d)
        return send(
            wg.at[lax.div(target, 2), lax.rem(target, 2)], got.at[me],
            (ss.at[d], sr.at[src]), tm=target,
        )

    def spot_of_sum():
        at = pl.multiple_of(lax.div(me, 2) * part_rows, part_rows)
        col = pl.multiple_of(half * part_cols, 128)
        return wsum.at[pl.ds(at, part_rows), pl.ds(col, part_cols)]

    def sum_copy(d, src):
        return send(red, spot_of_sum(), (gs.at[d], gr.at[src]), tm=ahead(d))

    for t in range(half_tiles):
        o_copy(t).wait_recv()
    turned = og[c].T
    for j in range(groups):
        part = jnp.dot(turned, cotv[j], preferred_element_type=f32).astype(bf)
        lanes = (j * wide) % part_cols
        wg[:, (j * wide) // part_cols, :, lanes : lanes + wide] = part.reshape(
            shards // 2, part_rows, wide
        )

    def start(d, carry):
        part_copy(d, me).start()
        return carry

    lax.fori_loop(1, shards, start, 0)
    o_far.start()
    o_near.start()
    got[pl.ds(me, 1)] = wg[lax.div(me, 2), pl.ds(half, 1)]
    leave(half_tiles)

    def arrive(d, carry):
        part_copy(d, behind(d)).wait_recv()
        return carry

    lax.fori_loop(1, shards, arrive, 0)

    def add(s, acc):
        return acc + got[s].astype(f32)

    red[...] = lax.fori_loop(0, shards, add, jnp.zeros(red.shape, f32)).astype(bf)
    o_far.wait_recv()
    o_relay.start()

    def start_sum(d, carry):
        sum_copy(d, me).start()
        return carry

    lax.fori_loop(1, shards, start_sum, 0)
    put = pltpu.make_async_copy(red, spot_of_sum(), os_.at[14])
    put.start()
    leave(half_tiles + 2)
    o_near.wait_recv()
    o_relay.wait_recv()
    for d in range(1, groups):
        w_copy(d, lax.rem(c + groups - d, groups)).wait()
    total = jnp.zeros((rows_here, wide), f32)
    for j in range(groups):
        total += jnp.dot(og[j], wcols[j], preferred_element_type=f32)
    joined[...] = total.astype(bf)
    put_dq.start()
    for t in range(half_tiles):
        o_copy(t).wait_send()
        dq_copy(t).wait()

    def end(d, carry):
        part_copy(d, behind(d)).wait_send()
        sum_copy(d, behind(d)).wait()
        return carry

    lax.fori_loop(1, shards, end, 0)
    put.wait()
    put_dq.wait()
    o_far.wait_send()
    o_near.wait_send()
    o_relay.wait_send()
    cot_far.wait_send()
    cot_near.wait_send()
    cot_relay.wait_send()
    q_copy.wait_send()
    b_copy.wait_send()
    g_copy.wait_send()

    def drain(d, carry):
        for copy in key_copies(lax.rem(me + d, shards), d, me):
            copy.wait_send()
        return carry

    def drain_halos(s, carry):
        for copy in halo_copies(s):
            copy.wait_send()
        return carry

    lax.fori_loop(1, shards, drain, 0)
    lax.fori_loop(0, shards, drain_halos, 0)


def step(tk, tv, sq, cot, ow, starts, ends, order, shards, groups):
    bf = jnp.bfloat16
    f32 = jnp.float32
    rows, wide = sq.shape
    piece = tk.shape[1]
    side = shards * piece
    window = 4 * side
    reach = side // TBLK
    L = 2 * F
    tiles = 2 * rows // F
    keys = (2 * reach + F // SBLK) * TBLK
    cols = groups * wide
    pr, pc = wide // (shards // 2), cols // 2
    dma = pltpu.SemaphoreType.DMA
    vmem = pl.BlockSpec(memory_space=pltpu.VMEM)
    return pl.pallas_call(
        functools.partial(step_kernel, shards, tiles),
        out_shape=(
            jax.ShapeDtypeStruct((rows, wide), bf),
            jax.ShapeDtypeStruct((rows, wide), bf),
            jax.ShapeDtypeStruct((wide, cols), bf),
        ),
        in_specs=[ANY] * 5 + [vmem] * 2 + [ANY],
        out_specs=(vmem, ANY, ANY),
        scratch_shapes=[
            pltpu.VMEM((2, shards, piece, 256), bf),
            pltpu.VMEM((shards, piece, 256), bf),
            pltpu.VMEM((shards, piece, 256), bf),
            pltpu.VMEM((window // 128, 128), jnp.int32),
            pltpu.VMEM((GROUP, side), bf),
            pltpu.VMEM((window, 384), bf),
            pltpu.VMEM((272, window), bf),
        ]
        + [pltpu.VMEM((keys, L), f32)] * 5
        + [pltpu.VMEM((keys, L), bf)] * 6
        + [
            pltpu.VMEM((L, 256), bf),
            pltpu.VMEM((L, 128), bf),
            pltpu.VMEM((L, 128), bf),
            pltpu.VMEM((groups, rows, wide), bf),
            pltpu.VMEM((wide, cols), bf),
            pltpu.VMEM((groups, wide, wide), bf),
            pltpu.VMEM((2, rows, 128), bf),
            pltpu.VMEM((2, rows, 128), bf),
            pltpu.VMEM((2, rows, 128), bf),
            pltpu.VMEM((8, 128), jnp.int32),
            pltpu.VMEM((2, 8, 128), jnp.int32),
            pltpu.SMEM((2, 8, 128), jnp.int32),
            pltpu.VMEM((rows, 128), bf),
            pltpu.VMEM((rows, 128), bf),
            pltpu.VMEM((rows, 128), bf),
            pltpu.VMEM((groups, rows, wide), bf),
            pltpu.VMEM((shards // 2, 2, pr, pc), bf),
            pltpu.VMEM((shards, pr, pc), bf),
            pltpu.VMEM((pr, pc), bf),
        ]
        + [dma((shards,))] * 12
        + [dma((tiles // 2,))] * 4
        + [dma((groups,))] * 2
        + [dma((6,))] * 3
        + [dma((15,))],
        compiler_params=pltpu.CompilerParams(
            collective_id=0, has_side_effects=True, vmem_limit_bytes=67043328
        ),
        name="step",
    )(tk, tv, sq, cot, ow, starts, ends, order)


def settle_kernel(joined, dq, wsum, joined_out, dq_out, w_out):
    joined_out[...] = joined[...]
    dq_out[...] = dq[...]
    w_out[...] = wsum[...].astype(jnp.float32)


def settle(joined, dq, wsum):
    steps = 2
    arrays = (joined, dq, wsum)
    specs = [
        pl.BlockSpec((x.shape[0] // steps, x.shape[1]), lambda i: (i, 0)) for x in arrays
    ]
    return pl.pallas_call(
        settle_kernel,
        grid=(steps,),
        in_specs=specs,
        out_specs=tuple(specs),
        out_shape=(
            jax.ShapeDtypeStruct(joined.shape, joined.dtype),
            jax.ShapeDtypeStruct(dq.shape, dq.dtype),
            jax.ShapeDtypeStruct(wsum.shape, jnp.float32),
        ),
        name="settle",
    )(joined, dq, wsum)


def on_device(
    student_query,
    teacher_key,
    teacher_value,
    clip_order,
    band_start,
    band_end,
    output_weight,
    cotangent,
):
    shards = lax.axis_size("tm")
    groups = lax.axis_size("clip")
    rows, wide = student_query.shape
    trows = teacher_key.shape[0]
    piece = trows // shards
    blocks = rows // SBLK

    return settle(
        *step(
            teacher_key.reshape(shards, piece, wide),
            teacher_value.reshape(shards, piece, wide),
            student_query, cotangent, output_weight,
            band_start.reshape(1, blocks), band_end.reshape(1, blocks),
            clip_order.reshape(-1, 128), shards, groups,
        )
    )


def solution(mesh):
    return jax.shard_map(
        on_device,
        mesh=mesh,
        in_specs=(
            P("tm", "clip"),
            P("tm", "clip"),
            P("tm", "clip"),
            P(),
            P("tm"),
            P("tm"),
            P("clip", None),
            P("tm", "clip"),
        ),
        out_specs=(P("tm", "clip"), P("tm", "clip"), P("clip", None)),
        check_vma=False,
    )
```

```python
import functools
import math

import jax
import jax.numpy as jnp
from jax import lax
from jax.experimental import pallas as pl
from jax.experimental.pallas import tpu as pltpu
from jax.sharding import PartitionSpec as P

HDIM = 64
SBLK = 32
TBLK = 128
F = 128
CH = 1536
SUB = 512
GROUP = 1024
FAR = -3e38
ANY = pl.BlockSpec(memory_space=pl.ANY)
MESH = pl.DeviceIdType.MESH


def greet(shards, bits, wait=True):
    me = lax.axis_index("tm")
    c = lax.axis_index("clip")
    barrier = pltpu.get_barrier_semaphore()

    def tell(d, carry):
        pl.semaphore_signal(
            barrier, inc=1, device_id={"tm": lax.rem(me + d, shards)}, device_id_type=MESH
        )
        return carry

    lax.fori_loop(1, shards, tell, 0)
    for bit in bits:
        pl.semaphore_signal(
            barrier, inc=1, device_id={"clip": flip(c, bit)}, device_id_type=MESH
        )
    if wait:
        pl.semaphore_wait(barrier, shards - 1 + len(bits))


def flip(c, bit):
    if bit == 3:
        return 3 - c
    return c + bit - 2 * bit * lax.rem(lax.div(c, bit), 2)


def one_hot_rows(row, hot, at, side, piece):
    lane = lax.broadcasted_iota(jnp.int32, (128, 128), 1)
    col = jnp.broadcast_to(row, (128, 128)).T
    spot = lax.div(col, side) * piece + lax.rem(col, piece)
    base = jnp.where(lax.rem(spot, 128) == lane, lax.div(spot, 128), -1)
    base = base.astype(jnp.float32).astype(jnp.bfloat16)
    one = jnp.bfloat16(1)
    for k in range(side // 128):
        hot[at : at + 128, k * 128 : (k + 1) * 128] = jnp.maximum(
            one - jnp.abs(base - jnp.bfloat16(k)), jnp.bfloat16(0)
        )


def send(src, dst, sems, **where):
    return pltpu.make_async_remote_copy(
        src_ref=src, dst_ref=dst, send_sem=sems[0], recv_sem=sems[1],
        device_id=where, device_id_type=MESH,
    )


def step_kernel(
    shards, tiles, tk, tv, sq, cot, ow, starts, ends, order,
    joined, dq, wsum,
    kvin, left, right, idx, hot, kv, kvt, s0, s1, p0, p1, p2, p3, p4, p5, qb, gb, gb2,
    cotv, wv, wcols, gv, qp, gp, bv, bp, band,
    o_send, dq_send, dq_own, og, wg, got, red,
    ks, kr, vs, vr, ls, lr, rs, rr, ss, sr, gs, gr,
    oss, osr, dss, dsr, ws, wr, cs, ms, fs, os_,
):
    f32 = jnp.float32
    bf = jnp.bfloat16
    me = lax.axis_index("tm")
    c = lax.axis_index("clip")
    half = lax.rem(me, 2)
    mate = flip(me, 1)
    pair = lax.div(me, 2)
    groups, rows_here, wide = cotv.shape
    near, far = flip(c, 1), flip(c, 2)
    prev = lax.rem(me + shards - 2, shards)
    after = lax.rem(me + 2, shards)
    L = 2 * F
    nb = F // SBLK
    per = CH // TBLK
    piece = tk.shape[1]
    side = shards * piece
    irows = side // 128
    blocks = F * tiles // SBLK
    half_blocks = blocks // 2
    half_tiles = tiles // 2
    reach = side // TBLK
    span = (2 * reach + nb) // per
    scores = (s0, s1)
    part_rows, part_cols = red.shape
    own_cols = pl.ds(pl.multiple_of(half * 128, 128), 128)
    mate_cols = pl.ds(pl.multiple_of((1 - half) * 128, 128), 128)
    bv[...] = jnp.zeros_like(bv)
    bv[0:1, 0:half_blocks] = starts[...]
    bv[1:2, 0:half_blocks] = ends[...]
    greet(shards, (1, 2, 3))

    def key_copies(target, slot, src):
        p = lax.div(target, 2)
        col = pl.multiple_of(lax.rem(target, 2) * 128, 128)
        return (
            send(
                tk.at[pl.ds(2 * p, 2), :, pl.ds(col, 128)],
                kvin.at[:, me, :, pl.ds(0, 128)], (ks.at[slot], kr.at[src]), tm=target,
            ),
            send(
                tv.at[pl.ds(2 * p, 2), :, pl.ds(col, 128)],
                kvin.at[:, me, :, pl.ds(128, 128)], (vs.at[slot], vr.at[src]), tm=target,
            ),
        )

    def halo_copies(s):
        return (
            send(kvin.at[0, s], right.at[s], (rs.at[s], rr.at[s]), tm=prev),
            send(kvin.at[1, s], left.at[s], (ls.at[s], lr.at[s]), tm=after),
        )

    def w_copy(d, src):
        target = lax.rem(c + d, groups)
        theirs = pl.multiple_of(target * wide, 128)
        return send(
            ow.at[:, pl.ds(theirs, wide)], wcols.at[c], (ws.at[d], wr.at[src]), clip=target
        )

    mine = pl.multiple_of(c * wide, 128)
    cot_far = send(cot, cotv.at[c], (cs.at[0], cs.at[1]), clip=far)
    cot_near = send(cot, cotv.at[c], (cs.at[2], cs.at[3]), clip=near)
    cot_relay = send(cotv.at[far], cotv.at[far], (cs.at[4], cs.at[5]), clip=near)
    q_copy = send(sq.at[:, mate_cols], qp.at[half], (ms.at[0], ms.at[1]), tm=mate)
    b_copy = send(bv, bp.at[half], (ms.at[2], ms.at[3]), tm=mate)
    g_copy = send(gv.at[1 - half], gp.at[half], (ms.at[4], ms.at[5]), tm=mate)

    def start_keys(d, carry):
        for copy in key_copies(lax.rem(me + d, shards), d, me):
            copy.start()
        return carry

    lax.fori_loop(1, shards, start_keys, 0)
    cot_far.start()
    cot_near.start()
    q_copy.start()
    b_copy.start()
    mine_kv = (
        pltpu.make_async_copy(
            tk.at[pl.ds(2 * pair, 2), :, own_cols], kvin.at[:, me, :, pl.ds(0, 128)], os_.at[0]
        ),
        pltpu.make_async_copy(
            tv.at[pl.ds(2 * pair, 2), :, own_cols], kvin.at[:, me, :, pl.ds(128, 128)], os_.at[1]
        ),
    )
    mine_cot = (
        pltpu.make_async_copy(cot, cotv.at[c], os_.at[2]),
        pltpu.make_async_copy(ow, wv, os_.at[3]),
    )
    get_idx = []
    for e in range(4):
        at = pl.multiple_of(lax.rem(2 * pair + shards - 1 + e, shards) * irows, irows)
        get_idx.append(
            pltpu.make_async_copy(
                order.at[pl.ds(at, irows)], idx.at[pl.ds(e * irows, irows)], os_.at[7 + e]
            )
        )
    mine_rest = (
        pltpu.make_async_copy(ow.at[:, pl.ds(mine, wide)], wcols.at[c], os_.at[4]),
        pltpu.make_async_copy(sq.at[:, own_cols], qp.at[half], os_.at[5]),
        pltpu.make_async_copy(bv, bp.at[half], os_.at[6]),
    ) + tuple(get_idx)
    for copy in mine_cot + mine_kv + mine_rest:
        copy.start()
    for copy in mine_kv:
        copy.wait()
    for copy in halo_copies(me):
        copy.start()
    for copy in mine_rest:
        copy.wait()

    def choose(slot, first):
        for r in range(GROUP // 128):
            one_hot_rows(
                idx[pl.ds(first + r, 1), :], hot.at[slot], r * 128, side, piece
            )

    def place(slot, src, first):
        rows = jnp.dot(
            hot[slot], src.reshape(side, 256), preferred_element_type=f32
        ).astype(bf)
        at = pl.multiple_of(first, GROUP)
        kv[pl.ds(at, GROUP), 0:128] = rows[:, 0:128]
        kv[pl.ds(at, GROUP), 256:384] = rows[:, 128:256]
        kvt[0:256, pl.ds(at, GROUP)] = rows.T

    slots = 2 * side // GROUP
    each = GROUP // 128

    def choose_own(j, carry):
        choose(j, irows + j * each)
        return carry

    def choose_halo(j, carry):
        choose(j, j * each + 2 * irows * lax.div(2 * j, slots))
        return carry

    def sort_own(j, carry):
        place(j, kvin[lax.div(2 * j, slots)], side + j * GROUP)
        return carry

    def sort_left(j, carry):
        place(j, left[...], j * GROUP)
        return carry

    def sort_right(j, carry):
        place(j, right[...], j * GROUP + 2 * side)
        return carry

    def forward(d, carry):
        s = lax.rem(me + shards - d, shards)
        for copy in key_copies(lax.rem(me + d, shards), d, s):
            copy.wait_recv()
        for copy in halo_copies(s):
            copy.start()
        return carry

    lax.fori_loop(0, slots, choose_own, 0)
    lax.fori_loop(1, 3, forward, 0)
    kvt[256:272, :] = jnp.ones((16, kvt.shape[1]), bf)
    lane = lax.broadcasted_iota(jnp.int32, (128, 128), 1)

    def mark(k, carry):
        at = pl.multiple_of(k * TBLK, TBLK)
        kv[pl.ds(at, TBLK), 128:256] = jnp.where(lane == k, 1.0, 0.0).astype(bf)
        return carry

    lax.fori_loop(0, 4 * reach, mark, 0)
    lax.fori_loop(3, shards, forward, 0)
    lax.fori_loop(0, slots, sort_own, 0)
    cot_far.wait_recv()
    cot_relay.start()
    lax.fori_loop(0, slots, choose_halo, 0)
    for copy in mine_cot:
        copy.wait()
    cot_near.wait_recv()
    cot_relay.wait_recv()
    nt = (((1,), (1,)), ((), ()))
    grad = jnp.zeros((rows_here, wide), f32)
    for j in range(groups):
        grad += lax.dot_general(
            cotv[j], wv[:, j * wide : (j + 1) * wide], nt, preferred_element_type=f32
        )
    gv[0] = grad[:, 0:128].astype(bf)
    gv[1] = grad[:, 128:256].astype(bf)

    def came_left(s, carry):
        halo_copies(s)[1].wait_recv()
        return carry

    def came_right(s, carry):
        halo_copies(s)[0].wait_recv()
        return carry

    lax.fori_loop(0, shards, came_left, 0)
    lax.fori_loop(0, slots // 2, sort_left, 0)
    g_copy.start()
    put_g = pltpu.make_async_copy(gv.at[half], gp.at[half], os_.at[11])
    put_g.start()
    for d in range(1, groups):
        w_copy(d, c).start()
    lax.fori_loop(0, shards, came_right, 0)
    lax.fori_loop(slots // 2, slots, sort_right, 0)
    q_copy.wait_recv()
    b_copy.wait_recv()
    get_band = pltpu.make_async_copy(bp, band, os_.at[12])
    get_band.start()
    get_band.wait()

    flane = lax.broadcasted_iota(jnp.int32, (F, 128), 1)
    zero = jnp.zeros((F, 128), bf)
    tops, deltas, invs = {}, {}, {}
    scale = 1.0 / math.sqrt(HDIM)

    def weights(t):
        return (p0, p1)[t % 2] if t < half_tiles else (p2, p3, p4, p5)[t - half_tiles]

    def tile_at(t):
        return lax.rem(t + (1 - half) * half_tiles, tiles)

    def frames(ref, t):
        at = pl.multiple_of(lax.rem(tile_at(t), half_tiles) * F, F)
        return ref[lax.div(tile_at(t), half_tiles), pl.ds(at, F), :]

    def split_heads(x):
        return jnp.where(flane < HDIM, x, zero), jnp.where(flane < HDIM, zero, x)

    def join_heads(x):
        x = x.T
        return jnp.where(flane < HDIM, x[0:F], x[F:L])

    def spot(t, k, u):
        return pl.multiple_of(tile_at(t) * (nb * TBLK) + k * CH + u * SUB, TBLK)

    def o_copy(t):
        part = pl.ds(t * F, F)
        return send(
            o_send.at[part], og.at[c, part, own_cols], (oss.at[t], osr.at[t]), tm=mate
        )

    def dq_copy(t):
        part = pl.ds(t * F, F)
        return send(
            dq_send.at[part], dq.at[part, own_cols], (dss.at[t], dsr.at[t]), tm=mate
        )

    for t in range(tiles + 1):
        do1, do2, do3 = t < tiles, t >= 1, 2 <= t < half_tiles + 2
        if do3:
            gb[0:F, :], gb[F:L, :] = split_heads(frames(gp, t - 2))
        if do1:
            q = frames(qp, t) * bf(1.0 / math.sqrt(HDIM))
            qb[0:F, 0:128], qb[F:L, 0:128] = split_heads(q)
            block = lax.broadcasted_iota(jnp.int32, (SBLK, 128), 1)
            row = lax.div(tile_at(t), half_tiles)
            col = lax.rem(tile_at(t), half_tiles) * nb
            base_block = pair * blocks
            for r in range(nb):
                at = reach + tile_at(t) * nb + r
                lo = jnp.maximum(at + band[row, 0, col + r], reach - base_block)
                hi = jnp.minimum(
                    at + band[row, 1, col + r], shards * half_blocks - 1 + reach - base_block
                )
                bias = jnp.where((block >= lo) & (block <= hi), 0.0, FAR).astype(bf)
                qb[r * SBLK : (r + 1) * SBLK, 128:256] = bias
                qb[F + r * SBLK : F + (r + 1) * SBLK, 128:256] = bias

        def body(k, carry):
            top, o, dqt = carry
            for u in range(CH // SUB):
                at = pl.multiple_of(k * CH + u * SUB, SUB)
                if do1:
                    base = spot(t, k, u)
                    s = lax.dot_general(
                        kv[pl.ds(base, SUB), 0:256], qb[...], nt, preferred_element_type=f32
                    )
                    scores[t % 2][pl.ds(at, SUB), :] = s
                    top = jnp.maximum(top, jnp.max(s.reshape(SUB // 8, 8, L), axis=0))
                if do2:
                    base = spot(t - 1, k, u)
                    s = scores[(t - 1) % 2][pl.ds(at, SUB), :].reshape(SUB // 8, 8, L)
                    e = jnp.exp(s - tops[t - 1][None]).reshape(SUB, L).astype(bf)
                    weights(t - 1)[pl.ds(at, SUB), :] = e
                    o = o + jnp.dot(kvt[128:272, pl.ds(base, SUB)], e, preferred_element_type=f32)
                if do3:
                    base = spot(t - 2, k, u)
                    e = weights(t - 2)[pl.ds(at, SUB), :].astype(f32).reshape(SUB // 8, 8, L)
                    d = lax.dot_general(
                        kv[pl.ds(base, SUB), 256:384], gb[...], nt, preferred_element_type=f32
                    ).reshape(SUB // 8, 8, L)
                    ds = (e * (d - deltas[t - 2][None])).reshape(SUB, L).astype(bf)
                    dqt = dqt + jnp.dot(
                        kvt[0:128, pl.ds(base, SUB)], ds, preferred_element_type=f32
                    )
            return top, o, dqt

        top, o, dqt = lax.fori_loop(
            0, span, body,
            (
                jnp.full((8, L), -jnp.inf, f32),
                jnp.zeros((144, L), f32),
                jnp.zeros((128, L), f32),
            ),
        )
        if t == 1:
            g_copy.wait_recv()
            put_g.wait()
        if 2 <= t < half_tiles + 2:
            o_copy(t - 2).start()
        if 3 <= t < half_tiles + 3:
            dq_copy(t - 3).start()
        if do3:
            out = join_heads(dqt * (invs[t - 2] * scale)).astype(bf)
            dq_send[(t - 2) * F : (t - 1) * F, :] = out
        if do2:
            inv = 1.0 / o[128:129]
            o = o[0:128] * inv
            out = join_heads(o).astype(bf)
            if t - 1 < half_tiles:
                o_send[(t - 1) * F : t * F, :] = out
            else:
                og[c, (t - 1 - half_tiles) * F : (t - half_tiles) * F, own_cols] = out
            grad = jnp.concatenate(split_heads(frames(gp, t - 1)), axis=0).astype(f32).T
            deltas[t - 1] = jnp.broadcast_to(jnp.sum(o * grad, axis=0, keepdims=True), (8, L))
            invs[t - 1] = inv
        if do1:
            tops[t] = jnp.broadcast_to(jnp.max(top, axis=0, keepdims=True), (8, L))

    def leave(first):
        pairs = ((first, gb), (first + 1, gb2))
        for t, ref in pairs:
            ref[0:F, :], ref[F:L, :] = split_heads(frames(gp, t))

        def body(k, carry):
            carry = list(carry)
            for u in range(CH // SUB):
                at = pl.multiple_of(k * CH + u * SUB, SUB)
                for i, (t, ref) in enumerate(pairs):
                    base = spot(t, k, u)
                    d = lax.dot_general(
                        kv[pl.ds(base, SUB), 256:384], ref[...], nt, preferred_element_type=f32
                    ).reshape(SUB // 8, 8, L)
                    e = weights(t)[pl.ds(at, SUB), :].astype(f32).reshape(SUB // 8, 8, L)
                    ds = (e * (d - deltas[t][None])).reshape(SUB, L).astype(bf)
                    carry[i] = carry[i] + jnp.dot(
                        kvt[0:128, pl.ds(base, SUB)], ds, preferred_element_type=f32
                    )
            return tuple(carry)

        sums = lax.fori_loop(0, span, body, (jnp.zeros((128, L), f32),) * 2)
        for (t, _), dqt in zip(pairs, sums):
            at = (t - half_tiles) * F
            dq_own[at : at + F, :] = join_heads(dqt * (invs[t] * scale)).astype(bf)

    o_far = send(og.at[c], og.at[c], (fs.at[0], fs.at[1]), clip=far)
    o_near = send(og.at[c], og.at[c], (fs.at[2], fs.at[3]), clip=near)
    o_relay = send(og.at[far], og.at[far], (fs.at[4], fs.at[5]), clip=near)
    put_dq = pltpu.make_async_copy(dq_own, dq.at[:, own_cols], os_.at[13])

    def ahead(d):
        return lax.rem(me + lax.rem(13 * d, shards), shards)

    def behind(d):
        return lax.rem(me + shards - lax.rem(13 * d, shards), shards)

    def part_copy(d, src):
        target = ahead(d)
        return send(
            wg.at[lax.div(target, 2), lax.rem(target, 2)], got.at[me],
            (ss.at[d], sr.at[src]), tm=target,
        )

    def spot_of_sum():
        at = pl.multiple_of(lax.div(me, 2) * part_rows, part_rows)
        col = pl.multiple_of(half * part_cols, 128)
        return wsum.at[pl.ds(at, part_rows), pl.ds(col, part_cols)]

    def sum_copy(d, src):
        return send(red, spot_of_sum(), (gs.at[d], gr.at[src]), tm=ahead(d))

    for t in range(half_tiles):
        o_copy(t).wait_recv()
    turned = og[c].T
    for j in range(groups):
        part = jnp.dot(turned, cotv[j], preferred_element_type=f32).astype(bf)
        lanes = (j * wide) % part_cols
        wg[:, (j * wide) // part_cols, :, lanes : lanes + wide] = part.reshape(
            shards // 2, part_rows, wide
        )

    def start(d, carry):
        part_copy(d, me).start()
        return carry

    lax.fori_loop(1, shards, start, 0)
    o_far.start()
    o_near.start()
    got[pl.ds(me, 1)] = wg[lax.div(me, 2), pl.ds(half, 1)]
    leave(half_tiles)

    def arrive(d, carry):
        part_copy(d, behind(d)).wait_recv()
        return carry

    lax.fori_loop(1, shards, arrive, 0)

    def add(s, acc):
        return acc + got[s].astype(f32)

    red[...] = lax.fori_loop(0, shards, add, jnp.zeros(red.shape, f32)).astype(bf)
    o_far.wait_recv()
    o_relay.start()

    def start_sum(d, carry):
        sum_copy(d, me).start()
        return carry

    lax.fori_loop(1, shards, start_sum, 0)
    put = pltpu.make_async_copy(red, spot_of_sum(), os_.at[14])
    put.start()
    leave(half_tiles + 2)
    o_near.wait_recv()
    o_relay.wait_recv()
    for d in range(1, groups):
        w_copy(d, lax.rem(c + groups - d, groups)).wait()
    total = jnp.zeros((rows_here, wide), f32)
    for j in range(groups):
        total += jnp.dot(og[j], wcols[j], preferred_element_type=f32)
    joined[...] = total.astype(bf)
    put_dq.start()
    for t in range(half_tiles):
        o_copy(t).wait_send()
        dq_copy(t).wait()

    def end(d, carry):
        part_copy(d, behind(d)).wait_send()
        sum_copy(d, behind(d)).wait()
        return carry

    lax.fori_loop(1, shards, end, 0)
    put.wait()
    put_dq.wait()
    o_far.wait_send()
    o_near.wait_send()
    o_relay.wait_send()
    cot_far.wait_send()
    cot_near.wait_send()
    cot_relay.wait_send()
    q_copy.wait_send()
    b_copy.wait_send()
    g_copy.wait_send()

    def drain(d, carry):
        for copy in key_copies(lax.rem(me + d, shards), d, me):
            copy.wait_send()
        return carry

    def drain_halos(s, carry):
        for copy in halo_copies(s):
            copy.wait_send()
        return carry

    lax.fori_loop(1, shards, drain, 0)
    lax.fori_loop(0, shards, drain_halos, 0)


def step(tk, tv, sq, cot, ow, starts, ends, order, shards, groups):
    bf = jnp.bfloat16
    f32 = jnp.float32
    rows, wide = sq.shape
    piece = tk.shape[1]
    side = shards * piece
    window = 4 * side
    reach = side // TBLK
    L = 2 * F
    tiles = 2 * rows // F
    keys = (2 * reach + F // SBLK) * TBLK
    cols = groups * wide
    pr, pc = wide // (shards // 2), cols // 2
    dma = pltpu.SemaphoreType.DMA
    vmem = pl.BlockSpec(memory_space=pltpu.VMEM)
    return pl.pallas_call(
        functools.partial(step_kernel, shards, tiles),
        out_shape=(
            jax.ShapeDtypeStruct((rows, wide), bf),
            jax.ShapeDtypeStruct((rows, wide), bf),
            jax.ShapeDtypeStruct((wide, cols), bf),
        ),
        in_specs=[ANY] * 5 + [vmem] * 2 + [ANY],
        out_specs=(vmem, ANY, ANY),
        scratch_shapes=[
            pltpu.VMEM((2, shards, piece, 256), bf),
            pltpu.VMEM((shards, piece, 256), bf),
            pltpu.VMEM((shards, piece, 256), bf),
            pltpu.VMEM((window // 128, 128), jnp.int32),
            pltpu.VMEM((2 * side // GROUP, GROUP, side), bf),
            pltpu.VMEM((window, 384), bf),
            pltpu.VMEM((272, window), bf),
        ]
        + [pltpu.VMEM((keys, L), f32)] * 2
        + [pltpu.VMEM((keys, L), bf)] * 6
        + [
            pltpu.VMEM((L, 256), bf),
            pltpu.VMEM((L, 128), bf),
            pltpu.VMEM((L, 128), bf),
            pltpu.VMEM((groups, rows, wide), bf),
            pltpu.VMEM((wide, cols), bf),
            pltpu.VMEM((groups, wide, wide), bf),
            pltpu.VMEM((2, rows, 128), bf),
            pltpu.VMEM((2, rows, 128), bf),
            pltpu.VMEM((2, rows, 128), bf),
            pltpu.VMEM((8, 128), jnp.int32),
            pltpu.VMEM((2, 8, 128), jnp.int32),
            pltpu.SMEM((2, 8, 128), jnp.int32),
            pltpu.VMEM((rows, 128), bf),
            pltpu.VMEM((rows, 128), bf),
            pltpu.VMEM((rows, 128), bf),
            pltpu.VMEM((groups, rows, wide), bf),
            pltpu.VMEM((shards // 2, 2, pr, pc), bf),
            pltpu.VMEM((shards, pr, pc), bf),
            pltpu.VMEM((pr, pc), bf),
        ]
        + [dma((shards,))] * 12
        + [dma((tiles // 2,))] * 4
        + [dma((groups,))] * 2
        + [dma((6,))] * 3
        + [dma((15,))],
        compiler_params=pltpu.CompilerParams(
            collective_id=0, has_side_effects=True, vmem_limit_bytes=67043328
        ),
        name="step",
    )(tk, tv, sq, cot, ow, starts, ends, order)


def settle_kernel(joined, dq, wsum, joined_out, dq_out, w_out):
    joined_out[...] = joined[...]
    dq_out[...] = dq[...]
    w_out[...] = wsum[...].astype(jnp.float32)


def settle(joined, dq, wsum):
    steps = 2
    arrays = (joined, dq, wsum)
    specs = [
        pl.BlockSpec((x.shape[0] // steps, x.shape[1]), lambda i: (i, 0)) for x in arrays
    ]
    return pl.pallas_call(
        settle_kernel,
        grid=(steps,),
        in_specs=specs,
        out_specs=tuple(specs),
        out_shape=(
            jax.ShapeDtypeStruct(joined.shape, joined.dtype),
            jax.ShapeDtypeStruct(dq.shape, dq.dtype),
            jax.ShapeDtypeStruct(wsum.shape, jnp.float32),
        ),
        name="settle",
    )(joined, dq, wsum)


def on_device(
    student_query,
    teacher_key,
    teacher_value,
    clip_order,
    band_start,
    band_end,
    output_weight,
    cotangent,
):
    shards = lax.axis_size("tm")
    groups = lax.axis_size("clip")
    rows, wide = student_query.shape
    trows = teacher_key.shape[0]
    piece = trows // shards
    blocks = rows // SBLK

    return settle(
        *step(
            teacher_key.reshape(shards, piece, wide),
            teacher_value.reshape(shards, piece, wide),
            student_query, cotangent, output_weight,
            band_start.reshape(1, blocks), band_end.reshape(1, blocks),
            clip_order.reshape(-1, 128), shards, groups,
        )
    )


def solution(mesh):
    return jax.shard_map(
        on_device,
        mesh=mesh,
        in_specs=(
            P("tm", "clip"),
            P("tm", "clip"),
            P("tm", "clip"),
            P(),
            P("tm"),
            P("tm"),
            P("clip", None),
            P("tm", "clip"),
        ),
        out_specs=(P("tm", "clip"), P("tm", "clip"), P("clip", None)),
        check_vma=False,
    )
```

```python
import functools
import math

import jax
import jax.numpy as jnp
from jax import lax
from jax.experimental import pallas as pl
from jax.experimental.pallas import tpu as pltpu
from jax.sharding import PartitionSpec as P

HDIM = 64
SBLK = 32
TBLK = 128
F = 128
CH = 1536
SUB = 512
GROUP = 1024
FAR = -3e38
ANY = pl.BlockSpec(memory_space=pl.ANY)
MESH = pl.DeviceIdType.MESH


def greet(shards, bits, wait=True):
    me = lax.axis_index("tm")
    c = lax.axis_index("clip")
    barrier = pltpu.get_barrier_semaphore()

    def tell(d, carry):
        pl.semaphore_signal(
            barrier, inc=1, device_id={"tm": lax.rem(me + d, shards)}, device_id_type=MESH
        )
        return carry

    lax.fori_loop(1, shards, tell, 0)
    for bit in bits:
        pl.semaphore_signal(
            barrier, inc=1, device_id={"clip": flip(c, bit)}, device_id_type=MESH
        )
    if wait:
        pl.semaphore_wait(barrier, shards - 1 + len(bits))


def flip(c, bit):
    if bit == 3:
        return 3 - c
    return c + bit - 2 * bit * lax.rem(lax.div(c, bit), 2)


def one_hot_rows(row, hot, at, side, piece):
    lane = lax.broadcasted_iota(jnp.int32, (128, 128), 1)
    col = jnp.broadcast_to(row, (128, 128)).T
    spot = lax.div(col, side) * piece + lax.rem(col, piece)
    base = jnp.where(lax.rem(spot, 128) == lane, lax.div(spot, 128), -1)
    base = base.astype(jnp.float32).astype(jnp.bfloat16)
    one = jnp.bfloat16(1)
    for k in range(side // 128):
        hot[at : at + 128, k * 128 : (k + 1) * 128] = jnp.maximum(
            one - jnp.abs(base - jnp.bfloat16(k)), jnp.bfloat16(0)
        )


def send(src, dst, sems, **where):
    return pltpu.make_async_remote_copy(
        src_ref=src, dst_ref=dst, send_sem=sems[0], recv_sem=sems[1],
        device_id=where, device_id_type=MESH,
    )


def step_kernel(
    shards, tiles, tk, tv, sq, cot, ow, starts, ends, order,
    joined, dq, wsum,
    kvin, left, right, idx, hot, kv, kvt, s0, s1, p0, p1, p2, p3, p4, p5, qb, gb, gb2,
    cotv, wv, wcols, gv, qp, gp, bv, bp, band,
    o_send, dq_send, dq_own, og, wg, got, red,
    ks, kr, vs, vr, ls, lr, rs, rr, ss, sr, gs, gr,
    oss, osr, dss, dsr, ws, wr, cs, ms, fs, os_,
):
    f32 = jnp.float32
    bf = jnp.bfloat16
    me = lax.axis_index("tm")
    c = lax.axis_index("clip")
    half = lax.rem(me, 2)
    mate = flip(me, 1)
    pair = lax.div(me, 2)
    groups, rows_here, wide = cotv.shape
    near, far = flip(c, 1), flip(c, 2)
    prev = lax.rem(me + shards - 2, shards)
    after = lax.rem(me + 2, shards)
    L = 2 * F
    nb = F // SBLK
    per = CH // TBLK
    piece = tk.shape[1]
    side = shards * piece
    irows = side // 128
    blocks = F * tiles // SBLK
    half_blocks = blocks // 2
    half_tiles = tiles // 2
    reach = side // TBLK
    span = (2 * reach + nb) // per
    scores = (s0, s1)
    part_rows, part_cols = red.shape
    own_cols = pl.ds(pl.multiple_of(half * 128, 128), 128)
    mate_cols = pl.ds(pl.multiple_of((1 - half) * 128, 128), 128)
    bv[...] = jnp.zeros_like(bv)
    bv[0:1, 0:half_blocks] = starts[...]
    bv[1:2, 0:half_blocks] = ends[...]
    greet(shards, (1, 2, 3))

    def key_copies(target, slot, src):
        p = lax.div(target, 2)
        col = pl.multiple_of(lax.rem(target, 2) * 128, 128)
        return (
            send(
                tk.at[pl.ds(2 * p, 2), :, pl.ds(col, 128)],
                kvin.at[:, me, :, pl.ds(0, 128)], (ks.at[slot], kr.at[src]), tm=target,
            ),
            send(
                tv.at[pl.ds(2 * p, 2), :, pl.ds(col, 128)],
                kvin.at[:, me, :, pl.ds(128, 128)], (vs.at[slot], vr.at[src]), tm=target,
            ),
        )

    def halo_copies(s):
        return (
            send(kvin.at[0, s], right.at[s], (rs.at[s], rr.at[s]), tm=prev),
            send(kvin.at[1, s], left.at[s], (ls.at[s], lr.at[s]), tm=after),
        )

    def w_copy(d, src):
        target = lax.rem(c + d, groups)
        theirs = pl.multiple_of(target * wide, 128)
        return send(
            ow.at[:, pl.ds(theirs, wide)], wcols.at[c], (ws.at[d], wr.at[src]), clip=target
        )

    mine = pl.multiple_of(c * wide, 128)
    cot_far = send(cot, cotv.at[c], (cs.at[0], cs.at[1]), clip=far)
    cot_near = send(cot, cotv.at[c], (cs.at[2], cs.at[3]), clip=near)
    cot_relay = send(cotv.at[far], cotv.at[far], (cs.at[4], cs.at[5]), clip=near)
    q_copy = send(sq.at[:, mate_cols], qp.at[half], (ms.at[0], ms.at[1]), tm=mate)
    b_copy = send(bv, bp.at[half], (ms.at[2], ms.at[3]), tm=mate)
    g_copy = send(gv.at[1 - half], gp.at[half], (ms.at[4], ms.at[5]), tm=mate)

    cot_far.start()
    cot_near.start()

    def start_keys(d, carry):
        for copy in key_copies(lax.rem(me + d, shards), d, me):
            copy.start()
        return carry

    lax.fori_loop(1, shards, start_keys, 0)
    q_copy.start()
    b_copy.start()
    mine_kv = (
        pltpu.make_async_copy(
            tk.at[pl.ds(2 * pair, 2), :, own_cols], kvin.at[:, me, :, pl.ds(0, 128)], os_.at[0]
        ),
        pltpu.make_async_copy(
            tv.at[pl.ds(2 * pair, 2), :, own_cols], kvin.at[:, me, :, pl.ds(128, 128)], os_.at[1]
        ),
    )
    mine_cot = (
        pltpu.make_async_copy(cot, cotv.at[c], os_.at[2]),
        pltpu.make_async_copy(ow, wv, os_.at[3]),
    )
    get_idx = []
    for e in range(4):
        at = pl.multiple_of(lax.rem(2 * pair + shards - 1 + e, shards) * irows, irows)
        get_idx.append(
            pltpu.make_async_copy(
                order.at[pl.ds(at, irows)], idx.at[pl.ds(e * irows, irows)], os_.at[7 + e]
            )
        )
    mine_rest = (
        pltpu.make_async_copy(ow.at[:, pl.ds(mine, wide)], wcols.at[c], os_.at[4]),
        pltpu.make_async_copy(sq.at[:, own_cols], qp.at[half], os_.at[5]),
        pltpu.make_async_copy(bv, bp.at[half], os_.at[6]),
    ) + tuple(get_idx)
    for copy in mine_cot + mine_kv + mine_rest:
        copy.start()
    for copy in mine_kv:
        copy.wait()
    for copy in halo_copies(me):
        copy.start()
    for copy in mine_rest:
        copy.wait()

    def choose(slot, first):
        for r in range(GROUP // 128):
            one_hot_rows(
                idx[pl.ds(first + r, 1), :], hot.at[slot], r * 128, side, piece
            )

    def place(slot, src, first):
        rows = jnp.dot(
            hot[slot], src.reshape(side, 256), preferred_element_type=f32
        ).astype(bf)
        at = pl.multiple_of(first, GROUP)
        kv[pl.ds(at, GROUP), 0:128] = rows[:, 0:128]
        kv[pl.ds(at, GROUP), 256:384] = rows[:, 128:256]
        kvt[0:256, pl.ds(at, GROUP)] = rows.T

    slots = 2 * side // GROUP
    each = GROUP // 128

    def choose_own(j, carry):
        choose(j, irows + j * each)
        return carry

    def choose_halo(j, carry):
        choose(j, j * each + 2 * irows * lax.div(2 * j, slots))
        return carry

    def sort_own(j, carry):
        place(j, kvin[lax.div(2 * j, slots)], side + j * GROUP)
        return carry

    def sort_left(j, carry):
        place(j, left[...], j * GROUP)
        return carry

    def sort_right(j, carry):
        place(j, right[...], j * GROUP + 2 * side)
        return carry

    def forward(d, carry):
        s = lax.rem(me + shards - d, shards)
        for copy in key_copies(lax.rem(me + d, shards), d, s):
            copy.wait_recv()
        for copy in halo_copies(s):
            copy.start()
        return carry

    cot_far.wait_recv()
    cot_relay.start()
    for copy in mine_cot:
        copy.wait()
    cot_near.wait_recv()
    cot_relay.wait_recv()
    nt = (((1,), (1,)), ((), ()))
    grad = jnp.zeros((rows_here, wide), f32)
    for j in range(groups):
        grad += lax.dot_general(
            cotv[j], wv[:, j * wide : (j + 1) * wide], nt, preferred_element_type=f32
        )
    gv[0] = grad[:, 0:128].astype(bf)
    gv[1] = grad[:, 128:256].astype(bf)

    lax.fori_loop(1, 3, forward, 0)
    g_copy.start()
    put_g = pltpu.make_async_copy(gv.at[half], gp.at[half], os_.at[11])
    put_g.start()
    kvt[256:272, :] = jnp.ones((16, kvt.shape[1]), bf)
    lane = lax.broadcasted_iota(jnp.int32, (128, 128), 1)

    def mark(k, carry):
        at = pl.multiple_of(k * TBLK, TBLK)
        kv[pl.ds(at, TBLK), 128:256] = jnp.where(lane == k, 1.0, 0.0).astype(bf)
        return carry

    lax.fori_loop(0, 4 * reach, mark, 0)
    lax.fori_loop(3, shards, forward, 0)
    lax.fori_loop(0, slots, choose_own, 0)
    lax.fori_loop(0, slots, sort_own, 0)
    lax.fori_loop(0, slots, choose_halo, 0)

    def came_left(s, carry):
        halo_copies(s)[1].wait_recv()
        return carry

    def came_right(s, carry):
        halo_copies(s)[0].wait_recv()
        return carry

    lax.fori_loop(0, shards, came_left, 0)
    lax.fori_loop(0, slots // 2, sort_left, 0)
    for d in range(1, groups):
        w_copy(d, c).start()
    lax.fori_loop(0, shards, came_right, 0)
    lax.fori_loop(slots // 2, slots, sort_right, 0)
    q_copy.wait_recv()
    b_copy.wait_recv()
    get_band = pltpu.make_async_copy(bp, band, os_.at[12])
    get_band.start()
    get_band.wait()

    flane = lax.broadcasted_iota(jnp.int32, (F, 128), 1)
    zero = jnp.zeros((F, 128), bf)
    tops, deltas, invs = {}, {}, {}
    scale = 1.0 / math.sqrt(HDIM)

    def weights(t):
        return (p0, p1)[t % 2] if t < half_tiles else (p2, p3, p4, p5)[t - half_tiles]

    def tile_at(t):
        return lax.rem(t + (1 - half) * half_tiles, tiles)

    def frames(ref, t):
        at = pl.multiple_of(lax.rem(tile_at(t), half_tiles) * F, F)
        return ref[lax.div(tile_at(t), half_tiles), pl.ds(at, F), :]

    def split_heads(x):
        return jnp.where(flane < HDIM, x, zero), jnp.where(flane < HDIM, zero, x)

    def join_heads(x):
        x = x.T
        return jnp.where(flane < HDIM, x[0:F], x[F:L])

    def spot(t, k, u):
        return pl.multiple_of(tile_at(t) * (nb * TBLK) + k * CH + u * SUB, TBLK)

    def o_copy(t):
        part = pl.ds(t * F, F)
        return send(
            o_send.at[part], og.at[c, part, own_cols], (oss.at[t], osr.at[t]), tm=mate
        )

    def dq_copy(t):
        part = pl.ds(t * F, F)
        return send(
            dq_send.at[part], dq.at[part, own_cols], (dss.at[t], dsr.at[t]), tm=mate
        )

    for t in range(tiles + 1):
        do1, do2, do3 = t < tiles, t >= 1, 2 <= t < half_tiles + 2
        if do3:
            gb[0:F, :], gb[F:L, :] = split_heads(frames(gp, t - 2))
        if do1:
            q = frames(qp, t) * bf(1.0 / math.sqrt(HDIM))
            qb[0:F, 0:128], qb[F:L, 0:128] = split_heads(q)
            block = lax.broadcasted_iota(jnp.int32, (SBLK, 128), 1)
            row = lax.div(tile_at(t), half_tiles)
            col = lax.rem(tile_at(t), half_tiles) * nb
            base_block = pair * blocks
            for r in range(nb):
                at = reach + tile_at(t) * nb + r
                lo = jnp.maximum(at + band[row, 0, col + r], reach - base_block)
                hi = jnp.minimum(
                    at + band[row, 1, col + r], shards * half_blocks - 1 + reach - base_block
                )
                bias = jnp.where((block >= lo) & (block <= hi), 0.0, FAR).astype(bf)
                qb[r * SBLK : (r + 1) * SBLK, 128:256] = bias
                qb[F + r * SBLK : F + (r + 1) * SBLK, 128:256] = bias

        def body(k, carry):
            top, o, dqt = carry
            for u in range(CH // SUB):
                at = pl.multiple_of(k * CH + u * SUB, SUB)
                if do1:
                    base = spot(t, k, u)
                    s = lax.dot_general(
                        kv[pl.ds(base, SUB), 0:256], qb[...], nt, preferred_element_type=f32
                    )
                    scores[t % 2][pl.ds(at, SUB), :] = s
                    top = jnp.maximum(top, jnp.max(s.reshape(SUB // 8, 8, L), axis=0))
                if do2:
                    base = spot(t - 1, k, u)
                    s = scores[(t - 1) % 2][pl.ds(at, SUB), :].reshape(SUB // 8, 8, L)
                    e = jnp.exp(s - tops[t - 1][None]).reshape(SUB, L).astype(bf)
                    weights(t - 1)[pl.ds(at, SUB), :] = e
                    o = o + jnp.dot(kvt[128:272, pl.ds(base, SUB)], e, preferred_element_type=f32)
                if do3:
                    base = spot(t - 2, k, u)
                    e = weights(t - 2)[pl.ds(at, SUB), :].astype(f32).reshape(SUB // 8, 8, L)
                    d = lax.dot_general(
                        kv[pl.ds(base, SUB), 256:384], gb[...], nt, preferred_element_type=f32
                    ).reshape(SUB // 8, 8, L)
                    ds = (e * (d - deltas[t - 2][None])).reshape(SUB, L).astype(bf)
                    dqt = dqt + jnp.dot(
                        kvt[0:128, pl.ds(base, SUB)], ds, preferred_element_type=f32
                    )
            return top, o, dqt

        top, o, dqt = lax.fori_loop(
            0, span, body,
            (
                jnp.full((8, L), -jnp.inf, f32),
                jnp.zeros((144, L), f32),
                jnp.zeros((128, L), f32),
            ),
        )
        if t == 1:
            g_copy.wait_recv()
            put_g.wait()
        if 2 <= t < half_tiles + 2:
            o_copy(t - 2).start()
        if 3 <= t < half_tiles + 3:
            dq_copy(t - 3).start()
        if do3:
            out = join_heads(dqt * (invs[t - 2] * scale)).astype(bf)
            dq_send[(t - 2) * F : (t - 1) * F, :] = out
        if do2:
            inv = 1.0 / o[128:129]
            o = o[0:128] * inv
            out = join_heads(o).astype(bf)
            if t - 1 < half_tiles:
                o_send[(t - 1) * F : t * F, :] = out
            else:
                og[c, (t - 1 - half_tiles) * F : (t - half_tiles) * F, own_cols] = out
            grad = jnp.concatenate(split_heads(frames(gp, t - 1)), axis=0).astype(f32).T
            deltas[t - 1] = jnp.broadcast_to(jnp.sum(o * grad, axis=0, keepdims=True), (8, L))
            invs[t - 1] = inv
        if do1:
            tops[t] = jnp.broadcast_to(jnp.max(top, axis=0, keepdims=True), (8, L))

    def leave(first):
        pairs = ((first, gb), (first + 1, gb2))
        for t, ref in pairs:
            ref[0:F, :], ref[F:L, :] = split_heads(frames(gp, t))

        def body(k, carry):
            carry = list(carry)
            for u in range(CH // SUB):
                at = pl.multiple_of(k * CH + u * SUB, SUB)
                for i, (t, ref) in enumerate(pairs):
                    base = spot(t, k, u)
                    d = lax.dot_general(
                        kv[pl.ds(base, SUB), 256:384], ref[...], nt, preferred_element_type=f32
                    ).reshape(SUB // 8, 8, L)
                    e = weights(t)[pl.ds(at, SUB), :].astype(f32).reshape(SUB // 8, 8, L)
                    ds = (e * (d - deltas[t][None])).reshape(SUB, L).astype(bf)
                    carry[i] = carry[i] + jnp.dot(
                        kvt[0:128, pl.ds(base, SUB)], ds, preferred_element_type=f32
                    )
            return tuple(carry)

        sums = lax.fori_loop(0, span, body, (jnp.zeros((128, L), f32),) * 2)
        for (t, _), dqt in zip(pairs, sums):
            at = (t - half_tiles) * F
            dq_own[at : at + F, :] = join_heads(dqt * (invs[t] * scale)).astype(bf)

    o_far = send(og.at[c], og.at[c], (fs.at[0], fs.at[1]), clip=far)
    o_near = send(og.at[c], og.at[c], (fs.at[2], fs.at[3]), clip=near)
    o_relay = send(og.at[far], og.at[far], (fs.at[4], fs.at[5]), clip=near)
    put_dq = pltpu.make_async_copy(dq_own, dq.at[:, own_cols], os_.at[13])

    def ahead(d):
        return lax.rem(me + lax.rem(13 * d, shards), shards)

    def behind(d):
        return lax.rem(me + shards - lax.rem(13 * d, shards), shards)

    def part_copy(d, src):
        target = ahead(d)
        return send(
            wg.at[lax.div(target, 2), lax.rem(target, 2)], got.at[me],
            (ss.at[d], sr.at[src]), tm=target,
        )

    def spot_of_sum():
        at = pl.multiple_of(lax.div(me, 2) * part_rows, part_rows)
        col = pl.multiple_of(half * part_cols, 128)
        return wsum.at[pl.ds(at, part_rows), pl.ds(col, part_cols)]

    def sum_copy(d, src):
        return send(red, spot_of_sum(), (gs.at[d], gr.at[src]), tm=ahead(d))

    for t in range(half_tiles):
        o_copy(t).wait_recv()
    turned = og[c].T
    for j in range(groups):
        part = jnp.dot(turned, cotv[j], preferred_element_type=f32).astype(bf)
        lanes = (j * wide) % part_cols
        wg[:, (j * wide) // part_cols, :, lanes : lanes + wide] = part.reshape(
            shards // 2, part_rows, wide
        )

    def start(d, carry):
        part_copy(d, me).start()
        return carry

    lax.fori_loop(1, shards, start, 0)
    o_far.start()
    o_near.start()
    got[pl.ds(me, 1)] = wg[lax.div(me, 2), pl.ds(half, 1)]
    leave(half_tiles)

    def arrive(d, carry):
        part_copy(d, behind(d)).wait_recv()
        return carry

    lax.fori_loop(1, shards, arrive, 0)

    def add(s, acc):
        return acc + got[s].astype(f32)

    red[...] = lax.fori_loop(0, shards, add, jnp.zeros(red.shape, f32)).astype(bf)
    o_far.wait_recv()
    o_relay.start()

    def start_sum(d, carry):
        sum_copy(d, me).start()
        return carry

    lax.fori_loop(1, shards, start_sum, 0)
    put = pltpu.make_async_copy(red, spot_of_sum(), os_.at[14])
    put.start()
    leave(half_tiles + 2)
    o_near.wait_recv()
    o_relay.wait_recv()
    for d in range(1, groups):
        w_copy(d, lax.rem(c + groups - d, groups)).wait()
    total = jnp.zeros((rows_here, wide), f32)
    for j in range(groups):
        total += jnp.dot(og[j], wcols[j], preferred_element_type=f32)
    joined[...] = total.astype(bf)
    put_dq.start()
    for t in range(half_tiles):
        o_copy(t).wait_send()
        dq_copy(t).wait()

    def end(d, carry):
        part_copy(d, behind(d)).wait_send()
        sum_copy(d, behind(d)).wait()
        return carry

    lax.fori_loop(1, shards, end, 0)
    put.wait()
    put_dq.wait()
    o_far.wait_send()
    o_near.wait_send()
    o_relay.wait_send()
    cot_far.wait_send()
    cot_near.wait_send()
    cot_relay.wait_send()
    q_copy.wait_send()
    b_copy.wait_send()
    g_copy.wait_send()

    def drain(d, carry):
        for copy in key_copies(lax.rem(me + d, shards), d, me):
            copy.wait_send()
        return carry

    def drain_halos(s, carry):
        for copy in halo_copies(s):
            copy.wait_send()
        return carry

    lax.fori_loop(1, shards, drain, 0)
    lax.fori_loop(0, shards, drain_halos, 0)


def step(tk, tv, sq, cot, ow, starts, ends, order, shards, groups):
    bf = jnp.bfloat16
    f32 = jnp.float32
    rows, wide = sq.shape
    piece = tk.shape[1]
    side = shards * piece
    window = 4 * side
    reach = side // TBLK
    L = 2 * F
    tiles = 2 * rows // F
    keys = (2 * reach + F // SBLK) * TBLK
    cols = groups * wide
    pr, pc = wide // (shards // 2), cols // 2
    dma = pltpu.SemaphoreType.DMA
    vmem = pl.BlockSpec(memory_space=pltpu.VMEM)
    return pl.pallas_call(
        functools.partial(step_kernel, shards, tiles),
        out_shape=(
            jax.ShapeDtypeStruct((rows, wide), bf),
            jax.ShapeDtypeStruct((rows, wide), bf),
            jax.ShapeDtypeStruct((wide, cols), bf),
        ),
        in_specs=[ANY] * 5 + [vmem] * 2 + [ANY],
        out_specs=(vmem, ANY, ANY),
        scratch_shapes=[
            pltpu.VMEM((2, shards, piece, 256), bf),
            pltpu.VMEM((shards, piece, 256), bf),
            pltpu.VMEM((shards, piece, 256), bf),
            pltpu.VMEM((window // 128, 128), jnp.int32),
            pltpu.VMEM((2 * side // GROUP, GROUP, side), bf),
            pltpu.VMEM((window, 384), bf),
            pltpu.VMEM((272, window), bf),
        ]
        + [pltpu.VMEM((keys, L), f32)] * 2
        + [pltpu.VMEM((keys, L), bf)] * 6
        + [
            pltpu.VMEM((L, 256), bf),
            pltpu.VMEM((L, 128), bf),
            pltpu.VMEM((L, 128), bf),
            pltpu.VMEM((groups, rows, wide), bf),
            pltpu.VMEM((wide, cols), bf),
            pltpu.VMEM((groups, wide, wide), bf),
            pltpu.VMEM((2, rows, 128), bf),
            pltpu.VMEM((2, rows, 128), bf),
            pltpu.VMEM((2, rows, 128), bf),
            pltpu.VMEM((8, 128), jnp.int32),
            pltpu.VMEM((2, 8, 128), jnp.int32),
            pltpu.SMEM((2, 8, 128), jnp.int32),
            pltpu.VMEM((rows, 128), bf),
            pltpu.VMEM((rows, 128), bf),
            pltpu.VMEM((rows, 128), bf),
            pltpu.VMEM((groups, rows, wide), bf),
            pltpu.VMEM((shards // 2, 2, pr, pc), bf),
            pltpu.VMEM((shards, pr, pc), bf),
            pltpu.VMEM((pr, pc), bf),
        ]
        + [dma((shards,))] * 12
        + [dma((tiles // 2,))] * 4
        + [dma((groups,))] * 2
        + [dma((6,))] * 3
        + [dma((15,))],
        compiler_params=pltpu.CompilerParams(
            collective_id=0, has_side_effects=True, vmem_limit_bytes=67043328
        ),
        name="step",
    )(tk, tv, sq, cot, ow, starts, ends, order)


def settle_kernel(joined, dq, wsum, joined_out, dq_out, w_out):
    joined_out[...] = joined[...]
    dq_out[...] = dq[...]
    w_out[...] = wsum[...].astype(jnp.float32)


def settle(joined, dq, wsum):
    steps = 2
    arrays = (joined, dq, wsum)
    specs = [
        pl.BlockSpec((x.shape[0] // steps, x.shape[1]), lambda i: (i, 0)) for x in arrays
    ]
    return pl.pallas_call(
        settle_kernel,
        grid=(steps,),
        in_specs=specs,
        out_specs=tuple(specs),
        out_shape=(
            jax.ShapeDtypeStruct(joined.shape, joined.dtype),
            jax.ShapeDtypeStruct(dq.shape, dq.dtype),
            jax.ShapeDtypeStruct(wsum.shape, jnp.float32),
        ),
        name="settle",
    )(joined, dq, wsum)


def on_device(
    student_query,
    teacher_key,
    teacher_value,
    clip_order,
    band_start,
    band_end,
    output_weight,
    cotangent,
):
    shards = lax.axis_size("tm")
    groups = lax.axis_size("clip")
    rows, wide = student_query.shape
    trows = teacher_key.shape[0]
    piece = trows // shards
    blocks = rows // SBLK

    return settle(
        *step(
            teacher_key.reshape(shards, piece, wide),
            teacher_value.reshape(shards, piece, wide),
            student_query, cotangent, output_weight,
            band_start.reshape(1, blocks), band_end.reshape(1, blocks),
            clip_order.reshape(-1, 128), shards, groups,
        )
    )


def solution(mesh):
    return jax.shard_map(
        on_device,
        mesh=mesh,
        in_specs=(
            P("tm", "clip"),
            P("tm", "clip"),
            P("tm", "clip"),
            P(),
            P("tm"),
            P("tm"),
            P("clip", None),
            P("tm", "clip"),
        ),
        out_specs=(P("tm", "clip"), P("tm", "clip"), P("clip", None)),
        check_vma=False,
    )
```
